128 devices in a mesh: wide: 32 (over z, y, core), narrow: 4 (over x).
Axes of the slice: x: 4, y: 4, z: 4, core: 2. Of those that a mesh axis runs over, the one named last changes fastest.
Arguments:
- frames: float32 [131072, 440], P(('wide', 'narrow')), may hold values from -8 to 8
- targets: float32 [131072, 2048], P(('wide', 'narrow')), may hold values from -7 to 7
- projection: float32 [128, 440, 512], P(('wide', 'narrow')), may hold values from -0.25 to 0.25
- phases: float32 [128, 512], P(('wide', 'narrow')), may hold values from 0 to 6.283185
- block_order: int32 [128], replicated, may hold values from 0 to 127, each once
Outputs:
- residual: float32 [131072, 2048], P(('wide', 'narrow'))
- weights: float32 [2, 512, 2048], replicated
The draws below stay inside these ranges and needn't reach their ends.
Inputs may be any that keep to these rules, and one draw needn't show every extreme that they name: `block_order`: a permutation; steps use its first 2 entries.
All inputs are finite; a program needn't handle non-finite values.
Results may differ from the reference program's by a relative error of at most 0.0003.
Values sent between devices are 32-bit elements; how exact they have to be, the bound alone decides.
A program may use at most 128 MiB of HBM per device.

```python
import jax
import jax.numpy as jnp
from jax import lax

DIM = 440
FEATS = 512
TARGETS = 2048
STEPS = 2
BLOCKS = 128
ROWS = 131072


def shared_labels(key):
    return jax.random.randint(jax.random.fold_in(key, 11), (ROWS,), 0, TARGETS)


def draw_frames(key, part):
    labels = shared_labels(key)
    centers = jax.random.normal(jax.random.fold_in(key, 12), (TARGETS, DIM), jnp.float32)
    noise = 0.5 * jax.random.normal(jax.random.fold_in(key, 13), (ROWS, DIM), jnp.float32)
    return jnp.clip(centers[labels] + noise, -8.0, 8.0)


def draw_targets(key, part):
    labels = shared_labels(key)
    onehot = (labels[:, None] == jnp.arange(TARGETS)[None, :]).astype(jnp.float32)
    noise = jnp.clip(0.5 * jax.random.normal(jax.random.fold_in(key, 14), (ROWS, TARGETS), jnp.float32), -2.5, 2.5)
    return 4.0 * (onehot - 1.0 / TARGETS) + noise


def block_scale(stream_key, dims, split, low, top_value):
    gain, own = 1.0, jax.random.fold_in(stream_key, 6)
    for dim, parts in split:
        heights = jnp.exp(jax.random.uniform(jax.random.fold_in(own, dim), (parts,), jnp.float32, low / len(split), top_value / len(split)))
        gain = gain * jnp.repeat(heights, dims[dim] // parts).reshape([-1 if axis == dim else 1 for axis in range(len(dims))])
    return gain


def normal_values(key, dims, scale, limit, pieces=(), kind=jnp.bfloat16):
    level = block_scale(key, dims, pieces, -0.22, 0.18) if pieces else 1.0
    result = jax.random.normal(key, dims, jnp.float32) * scale * level
    return jnp.minimum(jnp.maximum(result, -limit), limit).astype(kind)


def setup_inputs(seed: int = 0) -> dict:
    splits = jax.random.split(jax.random.key(seed), 6)
    return {
        "frames": draw_frames(jax.random.fold_in(splits[5], 71), 0),
        "targets": draw_targets(jax.random.fold_in(splits[5], 71), 0),
        "projection": normal_values(splits[2], (BLOCKS, DIM, FEATS), DIM ** -0.5, 0.25, ((0, 128),), jnp.float32),
        "phases": jnp.clip(6.283185 * jax.random.uniform(splits[3], (BLOCKS, FEATS), jnp.float32) ** block_scale(splits[3], (BLOCKS, FEATS), ((0, 128),), -0.2, 0.2), 0.0, 6.283185),
        "block_order": jax.random.permutation(splits[4], BLOCKS).astype(jnp.int32),
    }


def features_of(frames, block_proj, block_phase):
    inner = jnp.dot(frames.astype(jnp.float32), block_proj.astype(jnp.float32), precision=lax.Precision.HIGHEST, preferred_element_type=jnp.float32)
    return jnp.sqrt(2.0 / block_proj.shape[1]) * jnp.cos(inner + block_phase[None, :])

def solve_block(gram_sum, cross_sum):
    width = gram_sum.shape[0]
    damping = 0.1 * jnp.trace(gram_sum) / width
    factor = jnp.linalg.cholesky(gram_sum + damping * jnp.eye(width, dtype=gram_sum.dtype))
    return jax.scipy.linalg.cho_solve((factor, True), cross_sum)

def reference(frames, targets, projection, phases, block_order):
    residual = targets
    solved = []
    for step_index in range(STEPS):
        chosen = block_order[step_index]
        feats = features_of(frames, projection[chosen], phases[chosen])
        gram_sum = jnp.dot(feats.T.astype(jnp.float32), feats.astype(jnp.float32), precision=lax.Precision.HIGHEST, preferred_element_type=jnp.float32)
        cross_sum = jnp.dot(feats.T.astype(jnp.float32), residual.astype(jnp.float32), precision=lax.Precision.HIGHEST, preferred_element_type=jnp.float32)
        weights = solve_block(gram_sum, cross_sum)
        residual = residual - jnp.dot(feats.astype(jnp.float32), weights.astype(jnp.float32), precision=lax.Precision.HIGHEST, preferred_element_type=jnp.float32)
        solved.append(weights)
    return (residual, jnp.stack(solved))
```

```python
import functools

import jax
import jax.numpy as jnp
from jax import lax
from jax.experimental import pallas as pl
from jax.experimental.pallas import tpu as pltpu
from jax.sharding import PartitionSpec as P

STEPS = 2
FEATS = 512
MESH = pl.DeviceIdType.MESH
AXES = "xyz"
ORDERS = ("xyz", "yzx", "zxy")
HIGHEST = lax.Precision.HIGHEST
HIGH = lax.Precision.HIGH


def position():
    wide = lax.axis_index("wide")
    return {
        "x": lax.axis_index("narrow"),
        "y": lax.rem(lax.div(wide, 2), 4),
        "z": lax.div(wide, 8),
        "c": lax.rem(wide, 2),
    }


def device_of(pos):
    return ((pos["z"] * 4 + pos["y"]) * 2 + pos["c"], pos["x"])


def moved(pos, axis, step):
    new = dict(pos)
    if axis == "c":
        new["c"] = 1 - pos["c"]
    else:
        new[axis] = lax.rem(pos[axis] + step, 4)
    return new


def greet(pos):
    barrier = pltpu.get_barrier_semaphore()
    peers = [moved(pos, "c", 1)] + [moved(pos, a, d) for a in AXES for d in (1, 2, 3)]
    for peer in peers:
        pl.semaphore_signal(barrier, inc=1, device_id=device_of(peer), device_id_type=MESH)
    pl.semaphore_wait(barrier, len(peers))


def region(pos, fixed):
    return tuple(pos[a] if a in fixed else slice(None) for a in AXES)


def remote(src, dst, send, recv, peer):
    return pltpu.make_async_remote_copy(
        src_ref=src, dst_ref=dst, send_sem=send, recv_sem=recv,
        device_id=device_of(peer), device_id_type=MESH,
    )


def reduce_scatter(pos, part, lanes, first, second, third, sems, out_store):
    send, recv = sems
    landing = (first, second, third)
    sent = []
    sums = [None] * 3
    starts = [lo for lo, _ in lanes]
    for stage in range(3):
        copies = [[] for _ in ORDERS]
        for color, order in enumerate(ORDERS):
            lo, n = lanes[color]
            axis = order[stage]
            fixed = order[: stage + 1]
            for d in (1, 2, 3):
                peer = moved(pos, axis, d)
                src = part.at[region(peer, fixed) + (slice(None), pl.ds(lo, n))]
                copy = remote(
                    src, landing[stage][color].at[d - 1],
                    send.at[stage, color, d - 1], recv.at[stage, color, d - 1], peer,
                )
                copy.start()
                copies[color].append(copy)
                sent.append(copy)
        for color, order in enumerate(ORDERS):
            lo, n = lanes[color]
            for copy in copies[color]:
                copy.wait_recv()
            fixed = order[: stage + 1]
            at = region(pos, fixed) + (slice(None), pl.ds(lo, n))
            came = landing[stage][color]
            part[at] = part[at] + came[0] + came[1] + came[2]
    return sent


def all_gather(pos, whole, lanes, sems):
    send, recv = sems
    core = pos["c"]
    sent = []
    for stage in range(3):
        copies = []
        for color, order in enumerate(ORDERS):
            lo, n = lanes[color]
            axis = order[2 - stage]
            fixed = order[: 3 - stage]
            at = (core,) + region(pos, fixed) + (slice(None), pl.ds(lo, n))
            for d in (1, 2, 3):
                copy = remote(
                    whole.at[at], whole.at[at],
                    send.at[stage, color, d - 1], recv.at[stage, color, d - 1], moved(pos, axis, d),
                )
                copy.start()
                copies.append(copy)
                sent.append(copy)
        for copy in copies:
            copy.wait_recv()
    return sent


def pair_sum(pos, whole, came, part, send, recv):
    core = pos["c"]
    copy = remote(whole.at[1 - core], came, send, recv, moved(pos, "c", 1))
    copy.start()
    copy.wait_recv()

    @pl.loop(0, 4)
    def _(i):
        part[i] = whole[core, i] + came[i]

    return copy


def all_reduce_kernel(lanes, value, out, came, part, *rest):
    first, second, third = rest[0:3], rest[3:6], rest[6:9]
    rs_send, rs_recv, ag_send, ag_recv, pair_send, pair_recv = rest[9:]
    pos = position()
    greet(pos)
    sent = [pair_sum(pos, value, came, part, pair_send.at[0], pair_recv.at[0])]
    sent += reduce_scatter(pos, part, lanes, first, second, third, (rs_send, rs_recv), None)
    mine = (pos["x"], pos["y"], pos["z"])
    out[(pos["c"],) + mine] = part[mine]
    sent += all_gather(pos, out, lanes, (ag_send, ag_recv))
    last = remote(out.at[pos["c"]], out.at[pos["c"]], pair_send.at[1], pair_recv.at[1], moved(pos, "c", 1))
    last.start()
    last.wait_recv()
    for copy in sent + [last]:
        copy.wait_send()


def reduce_scatter_kernel(lanes, value, out, came, part, *rest):
    first, second, third = rest[0:3], rest[3:6], rest[6:9]
    rs_send, rs_recv, pair_send, pair_recv = rest[9:]
    pos = position()
    greet(pos)
    sent = [pair_sum(pos, value, came, part, pair_send.at[0], pair_recv.at[0])]
    sent += reduce_scatter(pos, part, lanes, first, second, third, (rs_send, rs_recv), None)
    out[...] = part[pos["x"], pos["y"], pos["z"]]
    for copy in sent:
        copy.wait_send()


def all_gather_kernel(lanes, value, out, ag_send, ag_recv, pair_send, pair_recv):
    pos = position()
    greet(pos)
    out[pos["c"], pos["x"], pos["y"], pos["z"]] = value[...]
    sent = all_gather(pos, out, lanes, (ag_send, ag_recv))
    last = remote(out.at[pos["c"]], out.at[pos["c"]], pair_send.at[0], pair_recv.at[0], moved(pos, "c", 1))
    last.start()
    last.wait_recv()
    for copy in sent + [last]:
        copy.wait_send()


def scratch_for(rows, lanes):
    width = sum(n for _, n in lanes)
    return [
        pltpu.VMEM((4, 4, 4, rows, width), jnp.float32),
        pltpu.VMEM((4, 4, 4, rows, width), jnp.float32),
        *[pltpu.VMEM((3, 4, 4, rows, n), jnp.float32) for _, n in lanes],
        *[pltpu.VMEM((3, 4, rows, n), jnp.float32) for _, n in lanes],
        *[pltpu.VMEM((3, rows, n), jnp.float32) for _, n in lanes],
    ]


SEMS = [pltpu.SemaphoreType.DMA((3, 3, 3)), pltpu.SemaphoreType.DMA((3, 3, 3))]
PAIR = [pltpu.SemaphoreType.DMA((2,)), pltpu.SemaphoreType.DMA((2,))]
IN_VMEM = pl.BlockSpec(memory_space=pltpu.VMEM)


def call(kernel, lanes, out_shape, scratch, cid, value):
    return pl.pallas_call(
        functools.partial(kernel, lanes),
        out_shape=jax.ShapeDtypeStruct(out_shape, jnp.float32),
        in_specs=[IN_VMEM],
        out_specs=IN_VMEM,
        scratch_shapes=scratch,
        compiler_params=pltpu.CompilerParams(
            collective_id=cid, has_side_effects=True, vmem_limit_bytes=58 << 20
        ),
    )(value)


def summed_everywhere(value, rows, lanes, cid):
    width = sum(n for _, n in lanes)
    shape = (2, 4, 4, 4, rows, width)
    out = call(
        all_reduce_kernel, lanes, shape, scratch_for(rows, lanes) + SEMS + SEMS + PAIR, cid,
        value.reshape(shape),
    )
    return out.reshape(128 * rows, width)


def summed_scattered(value, rows, lanes, cid):
    width = sum(n for _, n in lanes)
    shape = (2, 4, 4, 4, rows, width)
    return call(
        reduce_scatter_kernel, lanes, (rows, width), scratch_for(rows, lanes) + SEMS + PAIR, cid,
        value.reshape(shape),
    )


def gathered(value, rows, lanes, cid):
    width = sum(n for _, n in lanes)
    out = call(all_gather_kernel, lanes, (2, 4, 4, 4, rows, width), SEMS + PAIR, cid, value)
    return out.reshape(128 * rows, width)


def scaled_cosine(angle):
    turns = jnp.round(angle * 0.15915494309189535)
    half = (angle * 0.5 - turns * 3.140625) - turns * 9.67653589793e-4
    z = half * half
    poly = -2.50521083854e-8
    for coef in (2.75573192239e-6, -1.98412698413e-4, 8.33333333333e-3, -1.66666666667e-1):
        poly = poly * z + coef
    sine = half + half * (z * poly)
    return 0.0625 - 0.125 * (sine * sine)


def swept(mats):
    lane = lax.broadcasted_iota(jnp.int32, (1, 128), 1)
    row = lax.broadcasted_iota(jnp.int32, (8, 1), 0)

    def eight_pivots(_, mats):
        mats = list(mats)
        for j in (0, 2, 4, 6):
            for m, a in enumerate(mats):
                col1, col2 = a[:, j : j + 1], a[:, j + 1 : j + 2]
                row1, row2 = a[j : j + 1, :], a[j + 1 : j + 2, :]
                d11, d12 = a[j : j + 1, j : j + 1], a[j : j + 1, j + 1 : j + 2]
                d22 = a[j + 1 : j + 2, j + 1 : j + 2]
                inv = 1.0 / d11
                low = d12 * inv
                p22 = 1.0 / (d22 - d12 * low)
                p12 = -low * p22
                p11 = inv - low * p12
                u1 = p11 * row1 + p12 * row2
                u2 = p12 * row1 + p22 * row2
                u1 = jnp.where(lane == j, p11, jnp.where(lane == j + 1, p12, u1))
                u2 = jnp.where(lane == j, p12, jnp.where(lane == j + 1, p22, u2))
                rest = jnp.where((lane == j) | (lane == j + 1), 0.0, a)
                new = rest - col1 * u1 - col2 * u2
                top = jnp.where(row == j, u1, jnp.where(row == j + 1, u2, new[:8]))
                mats[m] = jnp.concatenate([top, new[8:]], axis=0)
        return tuple(
            pltpu.roll(jnp.concatenate([a[8:], a[:8]], axis=0), 120, 1) for a in mats
        )

    return lax.fori_loop(0, 16, eight_pivots, tuple(mats))


def invert_kernel(gram, inverse, strip):
    for m in range(STEPS):
        g = gram[m]
        eye = lax.broadcasted_iota(jnp.int32, g.shape, 0) == lax.broadcasted_iota(jnp.int32, g.shape, 1)
        trace = jnp.sum(jnp.where(eye, g, 0.0), keepdims=True)
        inverse[m] = jnp.where(eye, g + trace * (0.1 / FEATS), g)

    @pl.loop(0, FEATS // 128)
    def _(k):
        at = pl.ds(pl.multiple_of(k * 128, 128), 128)
        blocks = swept([inverse[m, at, at] for m in range(STEPS)])
        for m in range(STEPS):
            strip[m] = jnp.dot(blocks[m], inverse[m, at, :], precision=HIGHEST, preferred_element_type=jnp.float32)
            strip[m, :, at] = blocks[m]
        for m in range(STEPS):
            column = inverse[m, :, at]
            inverse[m, :, at] = jnp.zeros_like(column)
            inverse[m] = inverse[m] - jnp.dot(
                column, strip[m], precision=HIGHEST, preferred_element_type=jnp.float32
            )
            inverse[m, at, :] = strip[m]


def damped_inverses(grams):
    return pl.pallas_call(
        invert_kernel,
        out_shape=jax.ShapeDtypeStruct((STEPS, FEATS, FEATS), jnp.float32),
        in_specs=[IN_VMEM],
        out_specs=IN_VMEM,
        scratch_shapes=[pltpu.VMEM((STEPS, 128, FEATS), jnp.float32)],
        compiler_params=pltpu.CompilerParams(vmem_limit_bytes=58 << 20),
    )(grams)


def dot(left, right, precision, dims=((1,), (0,))):
    return lax.dot_general(
        left, right, (dims, ((), ())), precision=precision, preferred_element_type=jnp.float32
    )


def per_device(frames, targets, projection, phases, block_order):
    me = lax.axis_index("wide") * 4 + lax.axis_index("narrow")
    packed = jnp.concatenate([projection[0], phases, jnp.zeros((71, FEATS), jnp.float32)])
    kept = jnp.stack([jnp.where(block_order[s] == me, packed, 0.0) for s in range(STEPS)])
    blocks = summed_everywhere(kept, 8, ((0, 128), (128, 128), (256, 256)), 1).reshape(STEPS, 512, FEATS)
    proj = jnp.concatenate([blocks[0, :440], blocks[1, :440]], axis=1)
    phase = jnp.concatenate([blocks[0, 440], blocks[1, 440]])
    feats = scaled_cosine(dot(frames, proj, HIGHEST) + phase[None, :])
    first, second = feats[:, :FEATS], feats[:, FEATS:]
    left = dot(feats, first, HIGH, ((0,), (0,)))
    right = dot(second, second, HIGH, ((0,), (0,)))
    grams = jnp.concatenate([left, jnp.concatenate([right[:, :256], right[:, 256:]])], axis=1)
    grams = summed_everywhere(grams, 8, ((0, 256), (256, 256), (512, 256)), 2)
    gram0, between = grams[:FEATS, :FEATS], grams[FEATS:, :FEATS]
    gram1 = jnp.concatenate([grams[:FEATS, FEATS:], grams[FEATS:, FEATS:]], axis=1)
    cross = dot(targets, feats, HIGH, ((0,), (0,)))
    thirds = ((0, 384), (384, 384), (768, 256))
    cross = summed_scattered(cross, 16, thirds, 3)
    inverses = damped_inverses(jnp.stack([gram0, gram1]))
    w0 = dot(cross[:, :FEATS], inverses[0], HIGHEST)
    left_over = cross[:, FEATS:] - dot(w0, between, HIGHEST, ((1,), (1,)))
    w1 = dot(left_over, inverses[1], HIGHEST)
    solved = gathered(jnp.concatenate([w0, w1], axis=1), 16, thirds, 4)
    residual = targets - dot(feats, solved, HIGH, ((1,), (1,)))
    weights = jnp.stack([solved[:, :FEATS].T, solved[:, FEATS:].T])
    return (residual, weights)


def solution(mesh):
    return jax.shard_map(
        per_device,
        mesh=mesh,
        in_specs=(
            P(("wide", "narrow"), None),
            P(("wide", "narrow"), None),
            P(("wide", "narrow"), None, None),
            P(("wide", "narrow"), None),
            P(),
        ),
        out_specs=(P(("wide", "narrow"), None), P()),
        check_vma=False,
    )
```

```python
import jax
import jax.numpy as jnp
from jax import lax
from jax.experimental import pallas as pl
from jax.experimental.pallas import tpu as pltpu
from jax.sharding import PartitionSpec as P

STEPS = 2
FEATS = 512
MESH = pl.DeviceIdType.MESH
AXES = "xyz"
ORDERS = ("xyz", "yzx", "zxy")
HIGHEST = lax.Precision.HIGHEST
BF16 = jnp.bfloat16
F32 = jnp.float32
TN, NN, NT = ((0,), (0,)), ((1,), (0,)), ((1,), (1,))


def position():
    wide = lax.axis_index("wide")
    return {
        "x": lax.axis_index("narrow"),
        "y": lax.rem(lax.div(wide, 2), 4),
        "z": lax.div(wide, 8),
        "c": lax.rem(wide, 2),
    }


def device_of(pos):
    return ((pos["z"] * 4 + pos["y"]) * 2 + pos["c"], pos["x"])


def moved(pos, axis, step):
    new = dict(pos)
    if axis == "c":
        new["c"] = 1 - pos["c"]
    else:
        new[axis] = lax.rem(pos[axis] + step, 4)
    return new


def greet(pos):
    barrier = pltpu.get_barrier_semaphore()
    peers = [moved(pos, "c", 1)] + [moved(pos, a, d) for a in AXES for d in (1, 2, 3)]
    for peer in peers:
        pl.semaphore_signal(barrier, inc=1, device_id=device_of(peer), device_id_type=MESH)
    pl.semaphore_wait(barrier, len(peers))


def region(pos, fixed):
    return tuple(pos[a] if a in fixed else slice(None) for a in AXES)


def remote(src, dst, send, recv, peer):
    return pltpu.make_async_remote_copy(
        src_ref=src, dst_ref=dst, send_sem=send, recv_sem=recv,
        device_id=device_of(peer), device_id_type=MESH,
    )


def scatter_copies(pos, part, lanes, landing, sems, stage):
    send, recv = sems
    copies = []
    for color, order in enumerate(ORDERS):
        lo, n = lanes[color]
        for d in (1, 2, 3):
            peer = moved(pos, order[stage], d)
            src = part.at[region(peer, order[: stage + 1]) + (slice(None), pl.ds(lo, n))]
            copies.append(remote(
                src, landing[stage][color].at[d - 1],
                send.at[stage, color, d - 1], recv.at[stage, color, d - 1], peer,
            ))
    return copies


def scatter_start(*args):
    for copy in scatter_copies(*args):
        copy.start()


def scatter_finish(pos, part, lanes, landing, sems, stage):
    copies = scatter_copies(pos, part, lanes, landing, sems, stage)
    for color, order in enumerate(ORDERS):
        lo, n = lanes[color]
        for copy in copies[3 * color : 3 * color + 3]:
            copy.wait_recv()
        at = region(pos, order[: stage + 1]) + (slice(None), pl.ds(lo, n))
        came = landing[stage][color]
        part[at] = part[at] + came[0] + came[1] + came[2]


def gather_copies(pos, whole, lanes, sems, stage, own=None):
    send, recv = sems
    copies = []
    for color, order in enumerate(ORDERS):
        lo, n = lanes[color]
        at = region(pos, order[: 3 - stage]) + (slice(None), pl.ds(lo, n))
        src = whole.at[at] if own is None else own.at[:, pl.ds(lo, n)]
        for d in (1, 2, 3):
            copies.append(remote(
                src, whole.at[at],
                send.at[stage, color, d - 1], recv.at[stage, color, d - 1],
                moved(pos, order[2 - stage], d),
            ))
    return copies


def run_copies(copies):
    for copy in copies:
        copy.start()
    for copy in copies:
        copy.wait_recv()


def halves(x):
    high = x.astype(BF16)
    return high, (x - high.astype(F32)).astype(BF16)


def dot(left, right, dims=NN, precision=None):
    return lax.dot_general(
        left, right, (dims, ((), ())), precision=precision, preferred_element_type=F32
    )


def dot3(left, right, dims):
    (lh, ll), (rh, rl) = left, right
    return dot(lh, rh, dims) + dot(lh, rl, dims) + dot(ll, rh, dims)


def scaled_cosine(angle):
    turns = jnp.round(angle * 0.15915494309189535)
    half = (angle * 0.5 - turns * 3.140625) - turns * 9.67653589793e-4
    z = half * half
    poly = -2.50521083854e-8
    for coef in (2.75573192239e-6, -1.98412698413e-4, 8.33333333333e-3, -1.66666666667e-1):
        poly = poly * z + coef
    sine = half + half * (z * poly)
    return 0.0625 - 0.125 * (sine * sine)


def wide8(x):
    return jnp.broadcast_to(x, (8, 128))


def tree(terms):
    while len(terms) > 1:
        terms = [a + b for a, b in zip(terms[::2], terms[1::2])]
    return terms[0]


def eight_pivots(tiles, at):
    lane = lax.broadcasted_iota(jnp.int32, (8, 128), 1)
    row = lax.broadcasted_iota(jnp.int32, (8, 128), 0)
    top = tiles[at // 8]
    columns = [wide8(top[:, at + j : at + j + 1]) for j in range(8)]
    d = [[wide8(columns[j][i : i + 1, :]) for j in range(8)] for i in range(8)]
    for p in range(8):
        inv = 1.0 / d[p][p]
        scaled = [inv if j == p else d[p][j] * inv for j in range(8)]
        for i in range(8):
            if i != p:
                c = d[i][p]
                d[i] = [-c * inv if j == p else d[i][j] - c * scaled[j] for j in range(8)]
        d[p] = scaled
    packed = []
    for j in range(8):
        column = d[0][j]
        for i in range(1, 8):
            column = jnp.where(row == i, d[i][j], column)
        packed.append(column)
    new = tree([packed[j] * wide8(top[j : j + 1, :]) for j in range(8)])
    for j in range(8):
        new = jnp.where(lane == at + j, packed[j], new)
    rows = [wide8(new[j : j + 1, :]) for j in range(8)]
    inside = (lane >= at) & (lane < at + 8)
    out = []
    for t, tile in enumerate(tiles):
        if t == at // 8:
            out.append(new)
        else:
            change = tree([wide8(tile[:, at + j : at + j + 1]) * rows[j] for j in range(8)])
            out.append(jnp.where(inside, 0.0, tile) - change)
    return out


def inverse128(a):
    def quarter(_, a):
        tiles = [a[8 * t : 8 * t + 8] for t in range(16)]
        for k in range(4):
            tiles = eight_pivots(tiles, 8 * k)
        return pltpu.roll(jnp.concatenate(tiles[4:] + tiles[:4], axis=0), 96, 1)

    return lax.fori_loop(0, 4, quarter, a)


def invert_block_step(matrix, strip, k):
    at = pl.ds(pl.multiple_of(k * 128, 128), 128)
    block = inverse128(matrix[at, at])
    strip[...] = dot(block, matrix[at, :], NN, HIGHEST)
    strip[:, at] = block
    column = matrix[:, at]
    matrix[:, at] = jnp.zeros_like(column)
    matrix[...] = matrix[...] - dot(column, strip[...], NN, HIGHEST)
    matrix[at, :] = strip[...]


def fit_kernel(
    mask, frames, proj, phases, targets_hbm,
    solved_hbm, fh, fl,
    targets, kept, kept_came, blocks, gram, gram_came, gram_sum, matrix, other, between, between2, strip,
    cross, cross_came, own,
    b1, b2, b3, b4, b5, b6, b7, b8, b9, g1, g2, g3, g4, g5, g6, g7, g8, g9, c1, c2, c3, c4, c5, c6, c7, c8, c9,
    bs, br, bgs, bgr, gs, gr, ggs, ggr, cs, cr, cgs, cgr, pair_send, pair_recv, local,
):
    pos = position()
    core = pos["c"]
    twin = moved(pos, "c", 1)
    spot = (pos["x"], pos["y"], pos["z"])
    sent = []

    def pair(i, src, dst):
        return remote(src, dst, pair_send.at[i], pair_recv.at[i], twin)

    load = pltpu.make_async_copy(targets_hbm, targets, local.at[0])
    load.start()

    for s in range(STEPS):
        here = mask[s, 0:1, :] > 0.5
        kept[s, 0:3] = jnp.where(here, proj[0:384, :], 0.0).reshape(3, 4, 4, 8, FEATS)
        kept[s, 3, 0] = jnp.where(here, proj[384:416, :], 0.0).reshape(4, 8, FEATS)
        kept[s, 3, 1, 0:3] = jnp.where(here, proj[416:440, :], 0.0).reshape(3, 8, FEATS)
        kept[s, 3, 1, 3] = jnp.broadcast_to(jnp.where(here, phases[...], 0.0), (8, FEATS))
        kept[s, 3, 2:4] = jnp.zeros((2, 4, 8, FEATS), F32)
    greet(pos)
    thirds = ((0, 128), (128, 128), (256, 256))
    landing = ((b1, b2, b3), (b4, b5, b6), (b7, b8, b9))
    swap = pair(0, kept.at[1 - core], kept_came)
    swap.start()
    sent.append(swap)
    swap.wait_recv()
    kept[core] = kept[core] + kept_came[...]
    part = kept.at[core]
    for stage in range(3):
        scatter_start(pos, part, thirds, landing, (bs, br), stage)
        sent += scatter_copies(pos, part, thirds, landing, (bs, br), stage)
        scatter_finish(pos, part, thirds, landing, (bs, br), stage)
    blocks[(core,) + spot] = kept[(core,) + spot]
    for stage in range(3):
        copies = gather_copies(pos, blocks.at[core], thirds, (bgs, bgr), stage)
        run_copies(copies)
        sent += copies
    swap = pair(1, blocks.at[core], blocks.at[core])
    swap.start()
    sent.append(swap)
    swap.wait_recv()

    @pl.loop(0, 4)
    def _(i):
        rows = pl.ds(pl.multiple_of(i * 256, 256), 256)
        for s in range(STEPS):
            weights = blocks[s].reshape(512, FEATS)[:440]
            inner = dot(frames[rows, :], weights, NN, HIGHEST)
            high, low = halves(scaled_cosine(inner + blocks[s, 3, 1, 3, 0:1, :]))
            fh[rows, s * FEATS : (s + 1) * FEATS] = high
            fl[rows, s * FEATS : (s + 1) * FEATS] = low

    def feats(start, n):
        at = pl.ds(pl.multiple_of(start, 256), n)
        return fh[:, at], fl[:, at]

    def gram_half(c):
        @pl.loop(0, 2)
        def _(i):
            rows = pl.ds(i * 2, 2)
            square = dot3(feats(c * 512 + i * 256, 256), feats(c * 512, 512), TN)
            gram[c, rows, :, :, :, 0:512] = square.reshape(2, 4, 4, 8, 512)
            mixed = dot3(feats(512 + i * 256, 256), feats(c * 256, 256), TN)
            gram[c, rows, :, :, :, 512:768] = mixed.reshape(2, 4, 4, 8, 256)

    def cross_rows(c, lo, hi):
        @pl.loop(lo, hi)
        def _(i):
            at = pl.ds(pl.multiple_of(c * 1024 + i * 256, 256), 256)
            rows = dot3(halves(targets[:, at]), (fh[...], fl[...]), TN)
            cross[c, i] = rows.reshape(4, 4, 16, 1024)

    gram_half(1 - core)
    gram_swap = pair(2, gram.at[1 - core], gram_came)
    gram_swap.start()
    gram_half(core)
    load.wait()
    gram_swap.wait_recv()
    gram[core] = gram[core] + gram_came[...]
    part = gram.at[core]
    thirds = ((0, 256), (256, 256), (512, 256))
    landing = ((g1, g2, g3), (g4, g5, g6), (g7, g8, g9))
    args = (pos, part, thirds, landing, (gs, gr))
    scatter_start(*args, 0)
    cross_rows(1 - core, 0, 4)
    cross_swap = pair(3, cross.at[1 - core], cross_came)
    cross_swap.start()
    scatter_finish(*args, 0)
    scatter_start(*args, 1)
    cross_rows(core, 0, 2)
    scatter_finish(*args, 1)
    scatter_start(*args, 2)
    cross_rows(core, 2, 4)
    scatter_finish(*args, 2)
    for stage in range(3):
        sent += scatter_copies(*args, stage)
    gram_sum[spot] = gram[(core,) + spot]
    for stage in range(3):
        copies = gather_copies(pos, gram_sum, thirds, (ggs, ggr), stage)
        for copy in copies:
            copy.start()
        if stage == 0:
            cross_swap.wait_recv()

            @pl.loop(0, 4)
            def _(i):
                cross[core, i] = cross[core, i] + cross_came[i]

        for copy in copies:
            copy.wait_recv()
        sent += copies
    sent += [gram_swap, cross_swap]

    part = cross.at[core]
    thirds = ((0, 384), (384, 384), (768, 256))
    landing = ((c1, c2, c3), (c4, c5, c6), (c7, c8, c9))
    args = (pos, part, thirds, landing, (cs, cr))
    scatter_start(*args, 0)
    between[...] = gram_sum[:, :, :, :, 512:768].reshape(512, 256)
    mixed_swap = pair(4, between, between2)
    mixed_swap.start()
    square = gram_sum[:, :, :, :, 0:512].reshape(512, 512)
    eye = lax.broadcasted_iota(jnp.int32, square.shape, 0) == lax.broadcasted_iota(jnp.int32, square.shape, 1)
    trace = jnp.sum(jnp.where(eye, square, 0.0), keepdims=True)
    matrix[...] = jnp.where(eye, square + trace * (0.1 / FEATS), square)

    @pl.loop(0, 4)
    def _(k):
        invert_block_step(matrix, strip, k)

        @pl.when(k == 1)
        def _():
            scatter_finish(*args, 0)
            scatter_start(*args, 1)

        @pl.when(k == 2)
        def _():
            scatter_finish(*args, 1)
            scatter_start(*args, 2)

    inverse_swap = pair(5, matrix, other)
    inverse_swap.start()
    scatter_finish(*args, 2)
    for stage in range(3):
        sent += scatter_copies(*args, stage)
    sent += [mixed_swap, inverse_swap]

    mixed_swap.wait_recv()
    inverse_swap.wait_recv()
    mine = cross[(core,) + spot]
    first = core == 0
    inv0 = jnp.where(first, matrix[...], other[...])
    inv1 = jnp.where(first, other[...], matrix[...])
    low = jnp.where(first, between[...], between2[...])
    high = jnp.where(first, between2[...], between[...])
    w0 = dot(mine[:, :FEATS], inv0, NN, HIGHEST)
    seen = dot(w0[:, :256], low, NT, HIGHEST) + dot(w0[:, 256:], high, NT, HIGHEST)
    w1 = dot(mine[:, FEATS:] - seen, inv1, NN, HIGHEST)
    own[:, :FEATS] = w0
    own[:, FEATS:] = w1

    whole = solved_hbm.at[core]
    keep = pltpu.make_async_copy(own, whole.at[spot], local.at[1])
    keep.start()
    copies = gather_copies(pos, whole, thirds, (cgs, cgr), 0, own)
    run_copies(copies)
    keep.wait()
    sent += copies
    for stage in (1, 2):
        copies = gather_copies(pos, whole, thirds, (cgs, cgr), stage)
        run_copies(copies)
        sent += copies
    swap = pair(6, whole, whole)
    swap.start()
    swap.wait_recv()
    sent.append(swap)
    for copy in sent:
        copy.wait_send()


def landings(rows, widths):
    return [
        *[pltpu.VMEM((3, 4, 4, rows, n), F32) for n in widths],
        *[pltpu.VMEM((3, 4, rows, n), F32) for n in widths],
        *[pltpu.VMEM((3, rows, n), F32) for n in widths],
    ]


IN_VMEM = pl.BlockSpec(memory_space=pltpu.VMEM)
IN_HBM = pl.BlockSpec(memory_space=pl.ANY)


def fit(mask, frames, proj, phases, targets):
    return pl.pallas_call(
        fit_kernel,
        out_shape=(
            jax.ShapeDtypeStruct((2, 4, 4, 4, 16, 1024), F32),
            jax.ShapeDtypeStruct((1024, 1024), BF16),
            jax.ShapeDtypeStruct((1024, 1024), BF16),
        ),
        in_specs=[IN_VMEM, IN_VMEM, IN_VMEM, IN_VMEM, IN_HBM],
        out_specs=(IN_HBM, IN_VMEM, IN_VMEM),
        scratch_shapes=[
            pltpu.VMEM((1024, 2048), F32),
            pltpu.VMEM((2, 4, 4, 4, 8, FEATS), F32),
            pltpu.VMEM((4, 4, 4, 8, FEATS), F32),
            pltpu.VMEM((2, 4, 4, 4, 8, FEATS), F32),
            pltpu.VMEM((2, 4, 4, 4, 8, 768), F32),
            pltpu.VMEM((4, 4, 4, 8, 768), F32),
            pltpu.VMEM((4, 4, 4, 8, 768), F32),
            pltpu.VMEM((FEATS, FEATS), F32),
            pltpu.VMEM((FEATS, FEATS), F32),
            pltpu.VMEM((FEATS, 256), F32),
            pltpu.VMEM((FEATS, 256), F32),
            pltpu.VMEM((128, FEATS), F32),
            pltpu.VMEM((2, 4, 4, 4, 16, 1024), F32),
            pltpu.VMEM((4, 4, 4, 16, 1024), F32),
            pltpu.VMEM((16, 1024), F32),
            *landings(8, (128, 128, 256)),
            *landings(8, (256, 256, 256)),
            *landings(16, (384, 384, 256)),
            *[pltpu.SemaphoreType.DMA((3, 3, 3)) for _ in range(12)],
            pltpu.SemaphoreType.DMA((7,)),
            pltpu.SemaphoreType.DMA((7,)),
            pltpu.SemaphoreType.DMA((2,)),
        ],
        compiler_params=pltpu.CompilerParams(
            collective_id=1, has_side_effects=True, vmem_limit_bytes=60 << 20
        ),
    )(mask, frames, proj, phases, targets)


def residual_kernel(targets, solved, fh, fl, residual, weights):
    rows = solved[...]
    residual[...] = targets[...] - dot3((fh[...], fl[...]), halves(rows), NT)
    for s in range(STEPS):
        weights[s] = rows[:, s * FEATS : (s + 1) * FEATS].T


def residual_of(targets, solved, fh, fl):
    n = 256
    whole = pl.BlockSpec((1024, 1024), lambda i: (0, 0), pipeline_mode=pl.Buffered(1))
    return pl.pallas_call(
        residual_kernel,
        grid=(2048 // n,),
        out_shape=(
            jax.ShapeDtypeStruct((1024, 2048), F32),
            jax.ShapeDtypeStruct((STEPS, FEATS, 2048), F32),
        ),
        in_specs=[
            pl.BlockSpec((1024, n), lambda i: (0, i)),
            pl.BlockSpec((n, 1024), lambda i: (i, 0)),
            whole,
            whole,
        ],
        out_specs=(
            pl.BlockSpec((1024, n), lambda i: (0, i)),
            pl.BlockSpec((STEPS, FEATS, n), lambda i: (0, 0, i)),
        ),
        compiler_params=pltpu.CompilerParams(vmem_limit_bytes=48 << 20),
    )(targets, solved, fh, fl)


def per_device(frames, targets, projection, phases, block_order):
    me = lax.axis_index("wide") * 4 + lax.axis_index("narrow")
    mask = (block_order[:STEPS] == me).astype(F32)
    mask = jnp.broadcast_to(mask[:, None, None], (STEPS, 8, FEATS))
    solved, fh, fl = fit(mask, frames, projection[0], phases, targets)
    return residual_of(targets, solved.reshape(2048, 1024), fh, fl)


def solution(mesh):
    return jax.shard_map(
        per_device,
        mesh=mesh,
        in_specs=(
            P(("wide", "narrow"), None),
            P(("wide", "narrow"), None),
            P(("wide", "narrow"), None, None),
            P(("wide", "narrow"), None),
            P(),
        ),
        out_specs=(P(("wide", "narrow"), None), P()),
        check_vma=False,
    )
```

```python
import jax
import jax.numpy as jnp
from jax import lax
from jax.experimental import pallas as pl
from jax.experimental.pallas import tpu as pltpu
from jax.sharding import PartitionSpec as P

STEPS = 2
FEATS = 512
MESH = pl.DeviceIdType.MESH
AXES = "xyz"
ORDERS = ("xyz", "yzx", "zxy")
HIGHEST = lax.Precision.HIGHEST
BF16 = jnp.bfloat16
F32 = jnp.float32
TN, NN, NT = ((0,), (0,)), ((1,), (0,)), ((1,), (1,))


def position():
    wide = lax.axis_index("wide")
    return {
        "x": lax.axis_index("narrow"),
        "y": lax.rem(lax.div(wide, 2), 4),
        "z": lax.div(wide, 8),
        "c": lax.rem(wide, 2),
    }


def device_of(pos):
    return ((pos["z"] * 4 + pos["y"]) * 2 + pos["c"], pos["x"])


def moved(pos, axis, step):
    new = dict(pos)
    if axis == "c":
        new["c"] = 1 - pos["c"]
    else:
        new[axis] = lax.rem(pos[axis] + step, 4)
    return new


def greet(pos):
    barrier = pltpu.get_barrier_semaphore()
    peers = [moved(pos, "c", 1)] + [moved(pos, a, d) for a in AXES for d in (1, 2, 3)]
    for peer in peers:
        pl.semaphore_signal(barrier, inc=1, device_id=device_of(peer), device_id_type=MESH)
    return lambda: pl.semaphore_wait(barrier, len(peers))


def region(pos, fixed):
    return tuple(pos[a] if a in fixed else slice(None) for a in AXES)


def remote(src, dst, send, recv, peer):
    return pltpu.make_async_remote_copy(
        src_ref=src, dst_ref=dst, send_sem=send, recv_sem=recv,
        device_id=device_of(peer), device_id_type=MESH,
    )


def scatter_copies(pos, part, lanes, landing, sems, stage):
    send, recv = sems
    copies = []
    for color, order in enumerate(ORDERS):
        lo, n = lanes[color]
        for d in (1, 2, 3):
            peer = moved(pos, order[stage], d)
            src = part.at[region(peer, order[: stage + 1]) + (slice(None), pl.ds(lo, n))]
            copies.append(remote(
                src, landing[stage][color].at[d - 1],
                send.at[stage, color, d - 1], recv.at[stage, color, d - 1], peer,
            ))
    return copies


def scatter_start(*args):
    for copy in scatter_copies(*args):
        copy.start()


def scatter_finish(pos, part, lanes, landing, sems, stage):
    copies = scatter_copies(pos, part, lanes, landing, sems, stage)
    for color, order in enumerate(ORDERS):
        lo, n = lanes[color]
        for copy in copies[3 * color : 3 * color + 3]:
            copy.wait_recv()
        at = region(pos, order[: stage + 1]) + (slice(None), pl.ds(lo, n))
        came = landing[stage][color]
        part[at] = part[at] + came[0] + came[1] + came[2]


def gather_copies(pos, whole, lanes, sems, stage, own=None):
    send, recv = sems
    copies = []
    for color, order in enumerate(ORDERS):
        lo, n = lanes[color]
        at = region(pos, order[: 3 - stage]) + (slice(None), pl.ds(lo, n))
        src = whole.at[at] if own is None else own.at[:, pl.ds(lo, n)]
        for d in (1, 2, 3):
            copies.append(remote(
                src, whole.at[at],
                send.at[stage, color, d - 1], recv.at[stage, color, d - 1],
                moved(pos, order[2 - stage], d),
            ))
    return copies


def run_copies(copies):
    for copy in copies:
        copy.start()
    for copy in copies:
        copy.wait_recv()


def halves(x):
    high = x.astype(BF16)
    return high, (x - high.astype(F32)).astype(BF16)


def dot(left, right, dims=NN, precision=None):
    return lax.dot_general(
        left, right, (dims, ((), ())), precision=precision, preferred_element_type=F32
    )


def dot3(left, right, dims):
    (lh, ll), (rh, rl) = left, right
    return dot(lh, rh, dims) + dot(lh, rl, dims) + dot(ll, rh, dims)


def scaled_cosine(angle):
    turns = jnp.round(angle * 0.15915494309189535)
    half = (angle * 0.5 - turns * 3.140625) - turns * 9.67653589793e-4
    z = half * half
    poly = -2.50521083854e-8
    for coef in (2.75573192239e-6, -1.98412698413e-4, 8.33333333333e-3, -1.66666666667e-1):
        poly = poly * z + coef
    sine = half + half * (z * poly)
    return 0.0625 - 0.125 * (sine * sine)


def wide8(x):
    return jnp.broadcast_to(x, (8, 128))


def tree(terms):
    while len(terms) > 1:
        terms = [a + b for a, b in zip(terms[::2], terms[1::2])]
    return terms[0]


def eight_pivots(tiles, at):
    lane = lax.broadcasted_iota(jnp.int32, (8, 128), 1)
    row = lax.broadcasted_iota(jnp.int32, (8, 128), 0)
    top = tiles[at // 8]
    columns = [wide8(top[:, at + j : at + j + 1]) for j in range(8)]
    d = [[wide8(columns[j][i : i + 1, :]) for j in range(8)] for i in range(8)]
    for p in range(8):
        inv = 1.0 / d[p][p]
        scaled = [inv if j == p else d[p][j] * inv for j in range(8)]
        for i in range(8):
            if i != p:
                c = d[i][p]
                d[i] = [-c * inv if j == p else d[i][j] - c * scaled[j] for j in range(8)]
        d[p] = scaled
    packed = []
    for j in range(8):
        column = d[0][j]
        for i in range(1, 8):
            column = jnp.where(row == i, d[i][j], column)
        packed.append(column)
    new = tree([packed[j] * wide8(top[j : j + 1, :]) for j in range(8)])
    for j in range(8):
        new = jnp.where(lane == at + j, packed[j], new)
    rows = [wide8(new[j : j + 1, :]) for j in range(8)]
    inside = (lane >= at) & (lane < at + 8)
    out = []
    for t, tile in enumerate(tiles):
        if t == at // 8:
            out.append(new)
        else:
            change = tree([wide8(tile[:, at + j : at + j + 1]) * rows[j] for j in range(8)])
            out.append(jnp.where(inside, 0.0, tile) - change)
    return out


def inverse128(a, beside):
    def quarter(q, a):
        beside(q)
        tiles = [a[8 * t : 8 * t + 8] for t in range(16)]
        for k in range(4):
            tiles = eight_pivots(tiles, 8 * k)
        return pltpu.roll(jnp.concatenate(tiles[4:] + tiles[:4], axis=0), 96, 1)

    return lax.fori_loop(0, 4, quarter, a)


def block_at(k):
    return pl.ds(pl.multiple_of(k * 128, 128), 128)


def invert(matrix, strip, column, after_step):
    def update(q):
        rows = block_at(q)
        matrix[rows, :] = matrix[rows, :] - dot(column[rows, :], strip[...], NN, HIGHEST)

    def step(k, diagonal):
        at, following = block_at(k), block_at(lax.rem(k + 1, 4))
        block = inverse128(diagonal, update)
        strip[...] = dot(block, matrix[at, :], NN, HIGHEST)
        strip[:, at] = block
        column[...] = matrix[:, at]
        column[at, :] = jnp.zeros((128, 128), F32)
        matrix[:, at] = jnp.zeros((FEATS, 128), F32)
        matrix[at, :] = strip[...]
        after_step(k)
        return matrix[following, following] - dot(
            column[following, :], strip[:, following], NN, HIGHEST
        )

    strip[...] = jnp.zeros_like(strip)
    column[...] = jnp.zeros_like(column)
    lax.fori_loop(0, 4, step, matrix[block_at(0), block_at(0)])
    for q in range(4):
        update(q)


def fit_kernel(
    mask, proj, phases, frames_hbm, targets_hbm,
    solved_hbm, fh_hbm, fl_hbm,
    fh, fl, frames, frames_high, frames_low, proj_high, proj_low, targets, kept, kept_came, blocks, gram, gram_came, gram_sum, matrix, other, between, between2, strip, column,
    cross, cross_came, own,
    b1, b2, b3, b4, b5, b6, b7, b8, b9, g1, g2, g3, g4, g5, g6, g7, g8, g9, c1, c2, c3, c4, c5, c6, c7, c8, c9,
    bs, br, bgs, bgr, gs, gr, ggs, ggr, cs, cr, cgs, cgr, pair_send, pair_recv, fwd_send, fwd_recv, local,
):
    pos = position()
    core = pos["c"]
    twin = moved(pos, "c", 1)
    spot = (pos["x"], pos["y"], pos["z"])
    sent = []

    def pair(i, src, dst):
        return remote(src, dst, pair_send.at[i], pair_recv.at[i], twin)

    met = greet(pos)
    load_frames = pltpu.make_async_copy(frames_hbm, frames, local.at[2])
    load_frames.start()
    load = pltpu.make_async_copy(targets_hbm, targets, local.at[0])
    load.start()

    for s in range(STEPS):
        here = mask[s, 0:1, :] > 0.5
        kept[s, 0:3] = jnp.where(here, proj[0:384, :], 0.0).reshape(3, 4, 4, 8, FEATS)
        kept[s, 3, 0] = jnp.where(here, proj[384:416, :], 0.0).reshape(4, 8, FEATS)
        kept[s, 3, 1, 0:3] = jnp.where(here, proj[416:440, :], 0.0).reshape(3, 8, FEATS)
        kept[s, 3, 1, 3] = jnp.broadcast_to(jnp.where(here, phases[...], 0.0), (8, FEATS))
        kept[s, 3, 2:4] = jnp.zeros((2, 4, 8, FEATS), F32)
    met()
    thirds = ((0, 128), (128, 128), (256, 256))
    landing = ((b1, b2, b3), (b4, b5, b6), (b7, b8, b9))
    swap = pair(0, kept.at[1 - core], kept_came)
    swap.start()
    sent.append(swap)
    load_frames.wait()

    @pl.loop(0, 4)
    def _(i):
        at = pl.ds(pl.multiple_of(i * 256, 256), 256)
        high, low = halves(frames[:, at])
        frames_high[:, at] = high
        frames_low[:, at] = low

    swap.wait_recv()
    kept[core] = kept[core] + kept_came[...]
    part = kept.at[core]
    for stage in range(3):
        scatter_start(pos, part, thirds, landing, (bs, br), stage)
        sent += scatter_copies(pos, part, thirds, landing, (bs, br), stage)
        scatter_finish(pos, part, thirds, landing, (bs, br), stage)
    blocks[(core,) + spot] = kept[(core,) + spot]
    for stage in range(3):
        copies = gather_copies(pos, blocks.at[core], thirds, (bgs, bgr), stage)
        run_copies(copies)
        sent += copies
    swap = pair(1, blocks.at[core], blocks.at[core])
    swap.start()
    sent.append(swap)

    def features(s):
        high, low = halves(blocks[s].reshape(512, FEATS)[:440])
        proj_high[...] = high
        proj_low[...] = low
        lanes = pl.ds(pl.multiple_of(s * FEATS, FEATS), FEATS)

        @pl.loop(0, 4)
        def _(i):
            rows = pl.ds(pl.multiple_of(i * 256, 256), 256)
            inner = dot3(
                (frames_high[:, rows], frames_low[:, rows]), (proj_high[...], proj_low[...]), TN
            )
            high, low = halves(scaled_cosine(inner + blocks[s, 3, 1, 3, 0:1, :]))
            fh[rows, lanes] = high
            fl[rows, lanes] = low

    features(core)
    swap.wait_recv()
    features(1 - core)
    stores = [
        pltpu.make_async_copy(fh, fh_hbm, local.at[3]),
        pltpu.make_async_copy(fl, fl_hbm, local.at[4]),
    ]
    for store in stores:
        store.start()

    def feats(start, n):
        at = pl.ds(pl.multiple_of(start, 256), n)
        return fh[:, at], fl[:, at]

    def gram_half(c):
        @pl.loop(0, 2)
        def _(i):
            rows = pl.ds(i * 2, 2)
            square = dot3(feats(c * 512 + i * 256, 256), feats(c * 512, 512), TN)
            gram[c, rows, :, :, :, 0:512] = square.reshape(2, 4, 4, 8, 512)
            mixed = dot3(feats(512 + i * 256, 256), feats(c * 256, 256), TN)
            gram[c, rows, :, :, :, 512:768] = mixed.reshape(2, 4, 4, 8, 256)

    def cross_rows(c, lo, hi):
        @pl.loop(lo, hi)
        def _(i):
            at = pl.ds(pl.multiple_of(c * 1024 + i * 256, 256), 256)
            rows = dot3(halves(targets[:, at]), (fh[...], fl[...]), TN)
            cross[c, i] = rows.reshape(4, 4, 16, 1024)

    gram_half(1 - core)
    gram_swap = pair(2, gram.at[1 - core], gram_came)
    gram_swap.start()
    gram_half(core)
    load.wait()
    gram_swap.wait_recv()
    gram[core] = gram[core] + gram_came[...]
    part = gram.at[core]
    thirds = ((0, 256), (256, 256), (512, 256))
    landing = ((g1, g2, g3), (g4, g5, g6), (g7, g8, g9))
    args = (pos, part, thirds, landing, (gs, gr))
    scatter_start(*args, 0)
    cross_rows(1 - core, 0, 4)
    cross_swap = pair(3, cross.at[1 - core], cross_came)
    cross_swap.start()
    scatter_finish(*args, 0)
    scatter_start(*args, 1)
    cross_rows(core, 0, 2)
    scatter_finish(*args, 1)
    scatter_start(*args, 2)
    cross_rows(core, 2, 4)
    scatter_finish(*args, 2)
    for stage in range(3):
        sent += scatter_copies(*args, stage)
    gram_sum[spot] = gram[(core,) + spot]
    for stage in range(3):
        copies = gather_copies(pos, gram_sum, thirds, (ggs, ggr), stage)
        for copy in copies:
            copy.start()
        if stage == 0:
            cross_swap.wait_recv()

            @pl.loop(0, 4)
            def _(i):
                cross[core, i] = cross[core, i] + cross_came[i]

        for copy in copies:
            copy.wait_recv()
        sent += copies
    sent += [gram_swap, cross_swap]

    part = cross.at[core]
    thirds = ((0, 384), (384, 384), (768, 256))
    landing = ((c1, c2, c3), (c4, c5, c6), (c7, c8, c9))
    args = (pos, part, thirds, landing, (cs, cr))
    scatter_start(*args, 0)
    between[...] = gram_sum[:, :, :, :, 512:768].reshape(512, 256)
    mixed_swap = pair(4, between, between2)
    mixed_swap.start()
    square = gram_sum[:, :, :, :, 0:512].reshape(512, 512)
    eye = lax.broadcasted_iota(jnp.int32, square.shape, 0) == lax.broadcasted_iota(jnp.int32, square.shape, 1)
    trace = jnp.sum(jnp.where(eye, square, 0.0), keepdims=True)
    matrix[...] = jnp.where(eye, square + trace * (0.1 / FEATS), square)

    def after_step(k):
        @pl.when(k == 1)
        def _():
            scatter_finish(*args, 0)
            scatter_start(*args, 1)

        @pl.when(k == 2)
        def _():
            scatter_finish(*args, 1)
            scatter_start(*args, 2)

    invert(matrix, strip, column, after_step)

    inverse_swap = pair(5, matrix, other)
    inverse_swap.start()
    scatter_finish(*args, 2)
    for stage in range(3):
        sent += scatter_copies(*args, stage)
    sent += [mixed_swap, inverse_swap]

    mixed_swap.wait_recv()
    inverse_swap.wait_recv()
    mine = cross[(core,) + spot]
    first = core == 0
    inv0 = jnp.where(first, matrix[...], other[...])
    inv1 = jnp.where(first, other[...], matrix[...])
    low = jnp.where(first, between[...], between2[...])
    high = jnp.where(first, between2[...], between[...])
    w0 = dot(mine[:, :FEATS], inv0, NN, HIGHEST)
    seen = dot(w0[:, :256], low, NT, HIGHEST) + dot(w0[:, 256:], high, NT, HIGHEST)
    w1 = dot(mine[:, FEATS:] - seen, inv1, NN, HIGHEST)
    own[:, :FEATS] = w0
    own[:, FEATS:] = w1

    whole = solved_hbm.at[core]
    keep = pltpu.make_async_copy(own, whole.at[spot], local.at[1])
    keep.start()
    copies = gather_copies(pos, whole, thirds, (cgs, cgr), 0, own)
    run_copies(copies)
    keep.wait()
    sent += copies
    copies = gather_copies(pos, whole, thirds, (cgs, cgr), 1)
    run_copies(copies)
    sent += copies
    copies = gather_copies(pos, whole, thirds, (cgs, cgr), 2)
    for copy in copies:
        copy.start()
    sent += copies

    forwarded = []
    for d in (0, 1, 3, 2):
        for color, order in enumerate(ORDERS):
            lo, n = thirds[color]
            origin = pos
            if d:
                copies[3 * color + d - 1].wait_recv()
                origin = moved(pos, order[0], 4 - d)
            at = region(origin, order[:1]) + (slice(None), pl.ds(lo, n))
            copy = remote(whole.at[at], whole.at[at], fwd_send.at[color, d], fwd_recv.at[color, d], twin)
            copy.start()
            forwarded.append(copy)
    for copy in forwarded:
        copy.wait_recv()
    sent += forwarded
    for store in stores:
        store.wait()
    for copy in sent:
        copy.wait_send()


def landings(rows, widths):
    return [
        *[pltpu.VMEM((3, 4, 4, rows, n), F32) for n in widths],
        *[pltpu.VMEM((3, 4, rows, n), F32) for n in widths],
        *[pltpu.VMEM((3, rows, n), F32) for n in widths],
    ]


IN_VMEM = pl.BlockSpec(memory_space=pltpu.VMEM)
IN_HBM = pl.BlockSpec(memory_space=pl.ANY)


def fit(mask, proj, phases, frames, targets):
    return pl.pallas_call(
        fit_kernel,
        out_shape=(
            jax.ShapeDtypeStruct((2, 4, 4, 4, 16, 1024), F32),
            jax.ShapeDtypeStruct((1024, 1024), BF16),
            jax.ShapeDtypeStruct((1024, 1024), BF16),
        ),
        in_specs=[IN_VMEM, IN_VMEM, IN_VMEM, IN_HBM, IN_HBM],
        out_specs=(IN_HBM, IN_HBM, IN_HBM),
        scratch_shapes=[
            pltpu.VMEM((1024, 1024), BF16),
            pltpu.VMEM((1024, 1024), BF16),
            pltpu.VMEM((440, 1024), F32),
            pltpu.VMEM((440, 1024), BF16),
            pltpu.VMEM((440, 1024), BF16),
            pltpu.VMEM((440, FEATS), BF16),
            pltpu.VMEM((440, FEATS), BF16),
            pltpu.VMEM((1024, 2048), F32),
            pltpu.VMEM((2, 4, 4, 4, 8, FEATS), F32),
            pltpu.VMEM((4, 4, 4, 8, FEATS), F32),
            pltpu.VMEM((2, 4, 4, 4, 8, FEATS), F32),
            pltpu.VMEM((2, 4, 4, 4, 8, 768), F32),
            pltpu.VMEM((4, 4, 4, 8, 768), F32),
            pltpu.VMEM((4, 4, 4, 8, 768), F32),
            pltpu.VMEM((FEATS, FEATS), F32),
            pltpu.VMEM((FEATS, FEATS), F32),
            pltpu.VMEM((FEATS, 256), F32),
            pltpu.VMEM((FEATS, 256), F32),
            pltpu.VMEM((128, FEATS), F32),
            pltpu.VMEM((FEATS, 128), F32),
            pltpu.VMEM((2, 4, 4, 4, 16, 1024), F32),
            pltpu.VMEM((4, 4, 4, 16, 1024), F32),
            pltpu.VMEM((16, 1024), F32),
            *landings(8, (128, 128, 256)),
            *landings(8, (256, 256, 256)),
            *landings(16, (384, 384, 256)),
            *[pltpu.SemaphoreType.DMA((3, 3, 3)) for _ in range(12)],
            pltpu.SemaphoreType.DMA((6,)),
            pltpu.SemaphoreType.DMA((6,)),
            pltpu.SemaphoreType.DMA((3, 4)),
            pltpu.SemaphoreType.DMA((3, 4)),
            pltpu.SemaphoreType.DMA((5,)),
        ],
        compiler_params=pltpu.CompilerParams(
            collective_id=1, has_side_effects=True, vmem_limit_bytes=60 << 20
        ),
    )(mask, proj, phases, frames, targets)


def residual_kernel(targets, solved, fh, fl, residual, weights):
    rows = solved[...]
    residual[...] = targets[...] - dot3((fh[...], fl[...]), halves(rows), NT)
    for s in range(STEPS):
        weights[s] = rows[:, s * FEATS : (s + 1) * FEATS].T


def residual_of(targets, solved, fh, fl):
    n = 256
    return pl.pallas_call(
        residual_kernel,
        grid=(2048 // n,),
        out_shape=(
            jax.ShapeDtypeStruct((1024, 2048), F32),
            jax.ShapeDtypeStruct((STEPS, FEATS, 2048), F32),
        ),
        in_specs=[
            pl.BlockSpec((1024, n), lambda i: (0, i)),
            pl.BlockSpec((n, 1024), lambda i: (i, 0)),
            IN_VMEM,
            IN_VMEM,
        ],
        out_specs=(
            pl.BlockSpec((1024, n), lambda i: (0, i)),
            pl.BlockSpec((STEPS, FEATS, n), lambda i: (0, 0, i)),
        ),
        compiler_params=pltpu.CompilerParams(vmem_limit_bytes=60 << 20),
    )(targets, solved, fh, fl)


def per_device(frames, targets, projection, phases, block_order):
    me = lax.axis_index("wide") * 4 + lax.axis_index("narrow")
    mask = (block_order[:STEPS] == me).astype(F32)
    mask = jnp.broadcast_to(mask[:, None, None], (STEPS, 8, FEATS))
    solved, fh, fl = fit(mask, projection[0], phases, frames.T, targets)
    return residual_of(targets, solved.reshape(2048, 1024), fh, fl)


def solution(mesh):
    return jax.shard_map(
        per_device,
        mesh=mesh,
        in_specs=(
            P(("wide", "narrow"), None),
            P(("wide", "narrow"), None),
            P(("wide", "narrow"), None, None),
            P(("wide", "narrow"), None),
            P(),
        ),
        out_specs=(P(("wide", "narrow"), None), P()),
        check_vma=False,
    )
```

```python
import jax
import jax.numpy as jnp
from jax import lax
from jax.experimental import pallas as pl
from jax.experimental.pallas import tpu as pltpu
from jax.sharding import PartitionSpec as P

STEPS = 2
FEATS = 512
MESH = pl.DeviceIdType.MESH
AXES = "xyz"
ORDERS = ("xyz", "yzx", "zxy")
HIGHEST = lax.Precision.HIGHEST
BF16 = jnp.bfloat16
F32 = jnp.float32
TN, NN, NT = ((0,), (0,)), ((1,), (0,)), ((1,), (1,))


def position():
    wide = lax.axis_index("wide")
    return {
        "x": lax.axis_index("narrow"),
        "y": lax.rem(lax.div(wide, 2), 4),
        "z": lax.div(wide, 8),
        "c": lax.rem(wide, 2),
    }


def device_of(pos):
    return ((pos["z"] * 4 + pos["y"]) * 2 + pos["c"], pos["x"])


def moved(pos, axis, step):
    new = dict(pos)
    if axis == "c":
        new["c"] = 1 - pos["c"]
    else:
        new[axis] = lax.rem(pos[axis] + step, 4)
    return new


def greet(pos):
    barrier = pltpu.get_barrier_semaphore()
    peers = [moved(pos, "c", 1)] + [moved(pos, a, d) for a in AXES for d in (1, 2, 3)]
    for peer in peers:
        pl.semaphore_signal(barrier, inc=1, device_id=device_of(peer), device_id_type=MESH)
    return lambda: pl.semaphore_wait(barrier, len(peers))


def region(pos, fixed):
    return tuple(pos[a] if a in fixed else slice(None) for a in AXES)


def remote(src, dst, send, recv, peer):
    return pltpu.make_async_remote_copy(
        src_ref=src, dst_ref=dst, send_sem=send, recv_sem=recv,
        device_id=device_of(peer), device_id_type=MESH,
    )


def scatter_copies(pos, part, lanes, landing, sems, stage):
    send, recv = sems
    copies = []
    for color, order in enumerate(ORDERS):
        lo, n = lanes[color]
        for d in (1, 2, 3):
            peer = moved(pos, order[stage], d)
            src = part.at[region(peer, order[: stage + 1]) + (slice(None), pl.ds(lo, n))]
            copies.append(remote(
                src, landing[stage][color].at[d - 1],
                send.at[stage, color, d - 1], recv.at[stage, color, d - 1], peer,
            ))
    return copies


def scatter_start(*args):
    for copy in scatter_copies(*args):
        copy.start()


def scatter_finish(pos, part, lanes, landing, sems, stage):
    copies = scatter_copies(pos, part, lanes, landing, sems, stage)
    for color, order in enumerate(ORDERS):
        lo, n = lanes[color]
        for copy in copies[3 * color : 3 * color + 3]:
            copy.wait_recv()
        at = region(pos, order[: stage + 1]) + (slice(None), pl.ds(lo, n))
        came = landing[stage][color]
        part[at] = part[at] + came[0] + came[1] + came[2]


def gather_copies(pos, whole, lanes, sems, stage, own=None):
    send, recv = sems
    copies = []
    for color, order in enumerate(ORDERS):
        lo, n = lanes[color]
        at = region(pos, order[: 3 - stage]) + (slice(None), pl.ds(lo, n))
        src = whole.at[at] if own is None else own.at[:, pl.ds(lo, n)]
        for d in (1, 2, 3):
            copies.append(remote(
                src, whole.at[at],
                send.at[stage, color, d - 1], recv.at[stage, color, d - 1],
                moved(pos, order[2 - stage], d),
            ))
    return copies


def run_copies(copies):
    for copy in copies:
        copy.start()
    for copy in copies:
        copy.wait_recv()


def halves(x):
    high = x.astype(BF16)
    return high, (x - high.astype(F32)).astype(BF16)


def dot(left, right, dims=NN, precision=None):
    return lax.dot_general(
        left, right, (dims, ((), ())), precision=precision, preferred_element_type=F32
    )


def dot3(left, right, dims):
    (lh, ll), (rh, rl) = left, right
    return dot(lh, rh, dims) + dot(lh, rl, dims) + dot(ll, rh, dims)


def scaled_cosine(angle):
    turns = jnp.round(angle * 0.15915494309189535)
    half = (angle * 0.5 - turns * 3.140625) - turns * 9.67653589793e-4
    z = half * half
    poly = -2.50521083854e-8
    for coef in (2.75573192239e-6, -1.98412698413e-4, 8.33333333333e-3, -1.66666666667e-1):
        poly = poly * z + coef
    sine = half + half * (z * poly)
    return 0.0625 - 0.125 * (sine * sine)


def wide8(x):
    return jnp.broadcast_to(x, (8, 128))


def tree(terms):
    while len(terms) > 1:
        terms = [a + b for a, b in zip(terms[::2], terms[1::2])]
    return terms[0]


def eight_pivots(tiles, at):
    lane = lax.broadcasted_iota(jnp.int32, (8, 128), 1)
    row = lax.broadcasted_iota(jnp.int32, (8, 128), 0)
    top = tiles[at // 8]
    columns = [wide8(top[:, at + j : at + j + 1]) for j in range(8)]
    d = [[wide8(columns[j][i : i + 1, :]) for j in range(8)] for i in range(8)]
    for p in range(8):
        inv = 1.0 / d[p][p]
        scaled = [inv if j == p else d[p][j] * inv for j in range(8)]
        for i in range(8):
            if i != p:
                c = d[i][p]
                d[i] = [-c * inv if j == p else d[i][j] - c * scaled[j] for j in range(8)]
        d[p] = scaled
    packed = []
    for j in range(8):
        column = d[0][j]
        for i in range(1, 8):
            column = jnp.where(row == i, d[i][j], column)
        packed.append(column)
    new = tree([packed[j] * wide8(top[j : j + 1, :]) for j in range(8)])
    for j in range(8):
        new = jnp.where(lane == at + j, packed[j], new)
    rows = [wide8(new[j : j + 1, :]) for j in range(8)]
    inside = (lane >= at) & (lane < at + 8)
    out = []
    for t, tile in enumerate(tiles):
        if t == at // 8:
            out.append(new)
        else:
            change = tree([wide8(tile[:, at + j : at + j + 1]) * rows[j] for j in range(8)])
            out.append(jnp.where(inside, 0.0, tile) - change)
    return out


def inverse128(a, beside):
    def quarter(q, a):
        beside(q)
        tiles = [a[8 * t : 8 * t + 8] for t in range(16)]
        for k in range(4):
            tiles = eight_pivots(tiles, 8 * k)
        return pltpu.roll(jnp.concatenate(tiles[4:] + tiles[:4], axis=0), 96, 1)

    return lax.fori_loop(0, 4, quarter, a)


def block_at(k):
    return pl.ds(pl.multiple_of(k * 128, 128), 128)


def invert(matrix, strip, column, after_step, after_band):
    def update(q):
        rows = block_at(q)
        matrix[rows, :] = matrix[rows, :] - dot(column[rows, :], strip[...], NN, HIGHEST)

    def step(k, diagonal):
        at, following = block_at(k), block_at(lax.rem(k + 1, 4))
        block = inverse128(diagonal, update)
        strip[...] = dot(block, matrix[at, :], NN, HIGHEST)
        strip[:, at] = block
        column[...] = matrix[:, at]
        column[at, :] = jnp.zeros((128, 128), F32)
        matrix[:, at] = jnp.zeros((FEATS, 128), F32)
        matrix[at, :] = strip[...]
        after_step(k)
        return matrix[following, following] - dot(
            column[following, :], strip[:, following], NN, HIGHEST
        )

    strip[...] = jnp.zeros_like(strip)
    column[...] = jnp.zeros_like(column)
    lax.fori_loop(0, 4, step, matrix[block_at(0), block_at(0)])
    for q in range(4):
        update(q)
        after_band(q)


def fit_kernel(
    mask, proj, phases, frames_hbm, targets_hbm,
    solved_hbm, fh_hbm, fl_hbm,
    fh, fl, frames, frames_high, frames_low, proj_high, proj_low, targets, kept, kept_came, blocks, gram, gram_came, gram_sum, damped, inverses, mixed, strip, column,
    cross, cross_came, own,
    b1, b2, b3, b4, b5, b6, b7, b8, b9, g1, g2, g3, g4, g5, g6, g7, g8, g9, c1, c2, c3, c4, c5, c6, c7, c8, c9,
    bs, br, bgs, bgr, gs, gr, ggs, ggr, cs, cr, cgs, cgr, pair_send, pair_recv, fwd_send, fwd_recv, local,
):
    pos = position()
    core = pos["c"]
    twin = moved(pos, "c", 1)
    spot = (pos["x"], pos["y"], pos["z"])
    sent = []

    def pair(i, src, dst):
        return remote(src, dst, pair_send.at[i], pair_recv.at[i], twin)

    met = greet(pos)
    load_frames = pltpu.make_async_copy(frames_hbm, frames, local.at[2])
    load_frames.start()
    load = pltpu.make_async_copy(targets_hbm, targets, local.at[0])
    load.start()

    for s in range(STEPS):
        here = mask[s, 0:1, :] > 0.5
        kept[s, 0:3] = jnp.where(here, proj[0:384, :], 0.0).reshape(3, 4, 4, 8, FEATS)
        kept[s, 3, 0] = jnp.where(here, proj[384:416, :], 0.0).reshape(4, 8, FEATS)
        kept[s, 3, 1, 0:3] = jnp.where(here, proj[416:440, :], 0.0).reshape(3, 8, FEATS)
        kept[s, 3, 1, 3] = jnp.broadcast_to(jnp.where(here, phases[...], 0.0), (8, FEATS))
        kept[s, 3, 2:4] = jnp.zeros((2, 4, 8, FEATS), F32)
    met()
    thirds = ((0, 128), (128, 128), (256, 256))
    landing = ((b1, b2, b3), (b4, b5, b6), (b7, b8, b9))
    swap = pair(0, kept.at[1 - core], kept_came)
    swap.start()
    sent.append(swap)
    load_frames.wait()

    @pl.loop(0, 4)
    def _(i):
        at = pl.ds(pl.multiple_of(i * 256, 256), 256)
        high, low = halves(frames[:, at])
        frames_high[:, at] = high
        frames_low[:, at] = low

    swap.wait_recv()
    kept[core] = kept[core] + kept_came[...]
    part = kept.at[core]
    for stage in range(3):
        scatter_start(pos, part, thirds, landing, (bs, br), stage)
        sent += scatter_copies(pos, part, thirds, landing, (bs, br), stage)
        scatter_finish(pos, part, thirds, landing, (bs, br), stage)
    blocks[(core,) + spot] = kept[(core,) + spot]
    for stage in range(3):
        copies = gather_copies(pos, blocks.at[core], thirds, (bgs, bgr), stage)
        run_copies(copies)
        sent += copies
    swap = pair(1, blocks.at[core], blocks.at[core])
    swap.start()
    sent.append(swap)

    def features(s):
        high, low = halves(blocks[s].reshape(512, FEATS)[:440])
        proj_high[...] = high
        proj_low[...] = low
        lanes = pl.ds(pl.multiple_of(s * FEATS, FEATS), FEATS)

        for i in range(4):
            rows = slice(i * 256, i * 256 + 256)
            inner = dot3(
                (frames_high[:, rows], frames_low[:, rows]), (proj_high[...], proj_low[...]), TN
            )
            high, low = halves(scaled_cosine(inner + blocks[s, 3, 1, 3, 0:1, :]))
            fh[rows, lanes] = high
            fl[rows, lanes] = low

    features(core)
    swap.wait_recv()
    features(1 - core)
    stores = [
        pltpu.make_async_copy(fh, fh_hbm, local.at[3]),
        pltpu.make_async_copy(fl, fl_hbm, local.at[4]),
    ]
    for store in stores:
        store.start()

    def feats(start, n):
        at = pl.ds(pl.multiple_of(start, 256), n)
        return fh[:, at], fl[:, at]

    def gram_half(c):
        @pl.loop(0, 2)
        def _(i):
            rows = pl.ds(i * 2, 2)
            square = dot3(feats(c * 512 + i * 256, 256), feats(c * 512, 512), TN)
            gram[c, rows, :, :, :, 0:512] = square.reshape(2, 4, 4, 8, 512)
            mixed = dot3(feats(512 + i * 256, 256), feats(c * 256, 256), TN)
            gram[c, rows, :, :, :, 512:768] = mixed.reshape(2, 4, 4, 8, 256)

    def cross_rows(c, lo, hi):
        @pl.loop(lo, hi)
        def _(i):
            at = pl.ds(pl.multiple_of(c * 1024 + i * 256, 256), 256)
            rows = dot3(halves(targets[:, at]), (fh[...], fl[...]), TN)
            cross[c, i] = rows.reshape(4, 4, 16, 1024)

    gram_half(1 - core)
    gram_swap = pair(2, gram.at[1 - core], gram_came)
    gram_swap.start()
    gram_half(core)
    load.wait()
    gram_swap.wait_recv()
    gram[core] = gram[core] + gram_came[...]
    part = gram.at[core]
    thirds = ((0, 256), (256, 256), (512, 256))
    landing = ((g1, g2, g3), (g4, g5, g6), (g7, g8, g9))
    args = (pos, part, thirds, landing, (gs, gr))
    scatter_start(*args, 0)
    cross_rows(1 - core, 0, 4)
    cross_swap = pair(3, cross.at[1 - core], cross_came)
    cross_swap.start()
    scatter_finish(*args, 0)
    scatter_start(*args, 1)
    cross_rows(core, 0, 2)
    scatter_finish(*args, 1)
    scatter_start(*args, 2)
    cross_rows(core, 2, 4)
    scatter_finish(*args, 2)
    for stage in range(3):
        sent += scatter_copies(*args, stage)
    gram_sum[spot] = gram[(core,) + spot]
    for stage in range(3):
        copies = gather_copies(pos, gram_sum, thirds, (ggs, ggr), stage)
        for copy in copies:
            copy.start()
        if stage == 0:
            cross_swap.wait_recv()

            @pl.loop(0, 4)
            def _(i):
                cross[core, i] = cross[core, i] + cross_came[i]

        for copy in copies:
            copy.wait_recv()
        sent += copies
    sent += [gram_swap, cross_swap]

    part = cross.at[core]
    thirds = ((0, 384), (384, 384), (768, 256))
    landing = ((c1, c2, c3), (c4, c5, c6), (c7, c8, c9))
    args = (pos, part, thirds, landing, (cs, cr))
    scatter_start(*args, 0)
    mixed[core] = gram_sum[:, :, :, :, 512:768].reshape(512, 256)
    mixed_swap = pair(4, mixed.at[core], mixed.at[core])
    mixed_swap.start()
    square = gram_sum[:, :, :, :, 0:512].reshape(512, 512)
    eye = lax.broadcasted_iota(jnp.int32, square.shape, 0) == lax.broadcasted_iota(jnp.int32, square.shape, 1)
    trace = jnp.sum(jnp.where(eye, square, 0.0), keepdims=True)
    square = jnp.where(eye, square + trace * (0.1 / FEATS), square)
    damped[core] = square
    damped_swap = pair(5, damped.at[core], damped.at[core])
    damped_swap.start()
    matrix = inverses.at[core]
    matrix[...] = square

    def after_step(k):
        @pl.when(k == 1)
        def _():
            scatter_finish(*args, 0)
            scatter_start(*args, 1)

        @pl.when(k == 2)
        def _():
            scatter_finish(*args, 1)
            scatter_start(*args, 2)

    swaps = []

    def after_band(q):
        band = matrix.at[pl.ds(q * 128, 128)]
        swap = remote(band, band, fwd_send.at[3, q], fwd_recv.at[3, q], twin)
        swap.start()
        swaps.append(swap)

    invert(matrix, strip, column, after_step, after_band)

    scatter_finish(*args, 2)
    for stage in range(3):
        sent += scatter_copies(*args, stage)
    sent += [mixed_swap, damped_swap] + swaps

    mixed_swap.wait_recv()
    damped_swap.wait_recv()
    for swap in swaps:
        swap.wait_recv()
    mine = cross[(core,) + spot]

    def solve(step, right):
        guess = dot(right, inverses[step], NN, HIGHEST)
        left_over = right - dot(guess, damped[step], NN, HIGHEST)
        return guess + dot3(halves(left_over), halves(inverses[step]), NN)

    w0 = solve(0, mine[:, :FEATS])
    seen = dot(w0[:, :256], mixed[0], NT, HIGHEST) + dot(w0[:, 256:], mixed[1], NT, HIGHEST)
    w1 = solve(1, mine[:, FEATS:] - seen)
    own[:, :FEATS] = w0
    own[:, FEATS:] = w1

    whole = solved_hbm.at[core]
    keep = pltpu.make_async_copy(own, whole.at[spot], local.at[1])
    keep.start()
    copies = gather_copies(pos, whole, thirds, (cgs, cgr), 0, own)
    run_copies(copies)
    keep.wait()
    sent += copies
    copies = gather_copies(pos, whole, thirds, (cgs, cgr), 1)
    run_copies(copies)
    sent += copies
    copies = gather_copies(pos, whole, thirds, (cgs, cgr), 2)
    for copy in copies:
        copy.start()
    sent += copies

    forwarded = []
    for d in (0, 1, 3, 2):
        for color, order in enumerate(ORDERS):
            lo, n = thirds[color]
            origin = pos
            if d:
                copies[3 * color + d - 1].wait_recv()
                origin = moved(pos, order[0], 4 - d)
            at = region(origin, order[:1]) + (slice(None), pl.ds(lo, n))
            copy = remote(whole.at[at], whole.at[at], fwd_send.at[color, d], fwd_recv.at[color, d], twin)
            copy.start()
            forwarded.append(copy)
    for copy in forwarded:
        copy.wait_recv()
    sent += forwarded
    for store in stores:
        store.wait()
    for copy in sent:
        copy.wait_send()


def landings(rows, widths):
    return [
        *[pltpu.VMEM((3, 4, 4, rows, n), F32) for n in widths],
        *[pltpu.VMEM((3, 4, rows, n), F32) for n in widths],
        *[pltpu.VMEM((3, rows, n), F32) for n in widths],
    ]


IN_VMEM = pl.BlockSpec(memory_space=pltpu.VMEM)
IN_HBM = pl.BlockSpec(memory_space=pl.ANY)


def fit(mask, proj, phases, frames, targets):
    return pl.pallas_call(
        fit_kernel,
        out_shape=(
            jax.ShapeDtypeStruct((2, 4, 4, 4, 16, 1024), F32),
            jax.ShapeDtypeStruct((1024, 1024), BF16),
            jax.ShapeDtypeStruct((1024, 1024), BF16),
        ),
        in_specs=[IN_VMEM, IN_VMEM, IN_VMEM, IN_HBM, IN_HBM],
        out_specs=(IN_HBM, IN_HBM, IN_HBM),
        scratch_shapes=[
            pltpu.VMEM((1024, 1024), BF16),
            pltpu.VMEM((1024, 1024), BF16),
            pltpu.VMEM((440, 1024), F32),
            pltpu.VMEM((440, 1024), BF16),
            pltpu.VMEM((440, 1024), BF16),
            pltpu.VMEM((440, FEATS), BF16),
            pltpu.VMEM((440, FEATS), BF16),
            pltpu.VMEM((1024, 2048), F32),
            pltpu.VMEM((2, 4, 4, 4, 8, FEATS), F32),
            pltpu.VMEM((4, 4, 4, 8, FEATS), F32),
            pltpu.VMEM((2, 4, 4, 4, 8, FEATS), F32),
            pltpu.VMEM((2, 4, 4, 4, 8, 768), F32),
            pltpu.VMEM((4, 4, 4, 8, 768), F32),
            pltpu.VMEM((4, 4, 4, 8, 768), F32),
            pltpu.VMEM((STEPS, FEATS, FEATS), F32),
            pltpu.VMEM((STEPS, FEATS, FEATS), F32),
            pltpu.VMEM((2, FEATS, 256), F32),
            pltpu.VMEM((128, FEATS), F32),
            pltpu.VMEM((FEATS, 128), F32),
            pltpu.VMEM((2, 4, 4, 4, 16, 1024), F32),
            pltpu.VMEM((4, 4, 4, 16, 1024), F32),
            pltpu.VMEM((16, 1024), F32),
            *landings(8, (128, 128, 256)),
            *landings(8, (256, 256, 256)),
            *landings(16, (384, 384, 256)),
            *[pltpu.SemaphoreType.DMA((3, 3, 3)) for _ in range(12)],
            pltpu.SemaphoreType.DMA((6,)),
            pltpu.SemaphoreType.DMA((6,)),
            pltpu.SemaphoreType.DMA((4, 4)),
            pltpu.SemaphoreType.DMA((4, 4)),
            pltpu.SemaphoreType.DMA((5,)),
        ],
        compiler_params=pltpu.CompilerParams(
            collective_id=1, has_side_effects=True, vmem_limit_bytes=60 << 20
        ),
    )(mask, proj, phases, frames, targets)


def residual_kernel(targets, solved, fh, fl, residual, weights):
    rows = solved[...]
    residual[...] = targets[...] - dot3((fh[...], fl[...]), halves(rows), NT)
    for s in range(STEPS):
        weights[s] = rows[:, s * FEATS : (s + 1) * FEATS].T


def residual_of(targets, solved, fh, fl):
    n = 256
    return pl.pallas_call(
        residual_kernel,
        grid=(2048 // n,),
        out_shape=(
            jax.ShapeDtypeStruct((1024, 2048), F32),
            jax.ShapeDtypeStruct((STEPS, FEATS, 2048), F32),
        ),
        in_specs=[
            pl.BlockSpec((1024, n), lambda i: (0, i)),
            pl.BlockSpec((n, 1024), lambda i: (i, 0)),
            IN_VMEM,
            IN_VMEM,
        ],
        out_specs=(
            pl.BlockSpec((1024, n), lambda i: (0, i)),
            pl.BlockSpec((STEPS, FEATS, n), lambda i: (0, 0, i)),
        ),
        compiler_params=pltpu.CompilerParams(vmem_limit_bytes=60 << 20),
    )(targets, solved, fh, fl)


def per_device(frames, targets, projection, phases, block_order):
    me = lax.axis_index("wide") * 4 + lax.axis_index("narrow")
    mask = (block_order[:STEPS] == me).astype(F32)
    mask = jnp.broadcast_to(mask[:, None, None], (STEPS, 8, FEATS))
    solved, fh, fl = fit(mask, projection[0], phases, frames.T, targets)
    return residual_of(targets, solved.reshape(2048, 1024), fh, fl)


def solution(mesh):
    return jax.shard_map(
        per_device,
        mesh=mesh,
        in_specs=(
            P(("wide", "narrow"), None),
            P(("wide", "narrow"), None),
            P(("wide", "narrow"), None, None),
            P(("wide", "narrow"), None),
            P(),
        ),
        out_specs=(P(("wide", "narrow"), None), P()),
        check_vma=False,
    )
```

```python
import jax
import jax.numpy as jnp
from jax import lax
from jax.experimental import pallas as pl
from jax.experimental.pallas import tpu as pltpu
from jax.sharding import PartitionSpec as P

STEPS = 2
FEATS = 512
MESH = pl.DeviceIdType.MESH
AXES = "xyz"
ORDERS = ("xyz", "yzx", "zxy")
HIGHEST = lax.Precision.HIGHEST
BF16 = jnp.bfloat16
F32 = jnp.float32
TN, NN, NT = ((0,), (0,)), ((1,), (0,)), ((1,), (1,))


def position():
    wide = lax.axis_index("wide")
    return {
        "x": lax.axis_index("narrow"),
        "y": lax.rem(lax.div(wide, 2), 4),
        "z": lax.div(wide, 8),
        "c": lax.rem(wide, 2),
    }


def device_of(pos):
    return ((pos["z"] * 4 + pos["y"]) * 2 + pos["c"], pos["x"])


def moved(pos, axis, step):
    new = dict(pos)
    if axis == "c":
        new["c"] = 1 - pos["c"]
    else:
        new[axis] = lax.rem(pos[axis] + step, 4)
    return new


def greet(pos):
    barrier = pltpu.get_barrier_semaphore()
    peers = [moved(pos, "c", 1)] + [moved(pos, a, d) for a in AXES for d in (1, 2, 3)]
    for peer in peers:
        pl.semaphore_signal(barrier, inc=1, device_id=device_of(peer), device_id_type=MESH)
    return lambda: pl.semaphore_wait(barrier, len(peers))


def region(pos, fixed):
    return tuple(pos[a] if a in fixed else slice(None) for a in AXES)


def remote(src, dst, send, recv, peer):
    return pltpu.make_async_remote_copy(
        src_ref=src, dst_ref=dst, send_sem=send, recv_sem=recv,
        device_id=device_of(peer), device_id_type=MESH,
    )


def scatter_copies(pos, part, lanes, landing, sems, stage):
    send, recv = sems
    copies = []
    for color, order in enumerate(ORDERS):
        lo, n = lanes[color]
        for d in (1, 2, 3):
            peer = moved(pos, order[stage], d)
            src = part.at[region(peer, order[: stage + 1]) + (slice(None), pl.ds(lo, n))]
            copies.append(remote(
                src, landing[stage][color].at[d - 1],
                send.at[stage, color, d - 1], recv.at[stage, color, d - 1], peer,
            ))
    return copies


def scatter_start(*args):
    for copy in scatter_copies(*args):
        copy.start()


def scatter_finish(pos, part, lanes, landing, sems, stage):
    copies = scatter_copies(pos, part, lanes, landing, sems, stage)
    for color, order in enumerate(ORDERS):
        lo, n = lanes[color]
        for copy in copies[3 * color : 3 * color + 3]:
            copy.wait_recv()
        at = region(pos, order[: stage + 1]) + (slice(None), pl.ds(lo, n))
        came = landing[stage][color]
        part[at] = part[at] + came[0] + came[1] + came[2]


def gather_copies(pos, whole, lanes, sems, stage, own=None):
    send, recv = sems
    copies = []
    for color, order in enumerate(ORDERS):
        lo, n = lanes[color]
        at = region(pos, order[: 3 - stage]) + (slice(None), pl.ds(lo, n))
        src = whole.at[at] if own is None else own.at[:, pl.ds(lo, n)]
        for d in (1, 2, 3):
            copies.append(remote(
                src, whole.at[at],
                send.at[stage, color, d - 1], recv.at[stage, color, d - 1],
                moved(pos, order[2 - stage], d),
            ))
    return copies


def run_copies(copies):
    for copy in copies:
        copy.start()
    for copy in copies:
        copy.wait_recv()


def halves(x):
    high = x.astype(BF16)
    return high, (x - high.astype(F32)).astype(BF16)


def dot(left, right, dims=NN, precision=None):
    return lax.dot_general(
        left, right, (dims, ((), ())), precision=precision, preferred_element_type=F32
    )


def dot3(left, right, dims):
    (lh, ll), (rh, rl) = left, right
    return dot(lh, rh, dims) + dot(lh, rl, dims) + dot(ll, rh, dims)


def scaled_cosine(angle):
    turns = jnp.round(angle * 0.15915494309189535)
    half = (angle * 0.5 - turns * 3.140625) - turns * 9.67653589793e-4
    z = half * half
    poly = -2.50521083854e-8
    for coef in (2.75573192239e-6, -1.98412698413e-4, 8.33333333333e-3, -1.66666666667e-1):
        poly = poly * z + coef
    sine = half + half * (z * poly)
    return 0.0625 - 0.125 * (sine * sine)


def wide8(x):
    return jnp.broadcast_to(x, (8, 128))


def tree(terms):
    while len(terms) > 1:
        terms = [a + b for a, b in zip(terms[::2], terms[1::2])]
    return terms[0]


def eight_pivots(tiles, at):
    lane = lax.broadcasted_iota(jnp.int32, (8, 128), 1)
    row = lax.broadcasted_iota(jnp.int32, (8, 128), 0)
    top = tiles[at // 8]
    columns = [wide8(top[:, at + j : at + j + 1]) for j in range(8)]
    d = [[wide8(columns[j][i : i + 1, :]) for j in range(8)] for i in range(8)]
    for p in range(8):
        inv = 1.0 / d[p][p]
        scaled = [inv if j == p else d[p][j] * inv for j in range(8)]
        for i in range(8):
            if i != p:
                c = d[i][p]
                d[i] = [-c * inv if j == p else d[i][j] - c * scaled[j] for j in range(8)]
        d[p] = scaled
    packed = []
    for j in range(8):
        column = d[0][j]
        for i in range(1, 8):
            column = jnp.where(row == i, d[i][j], column)
        packed.append(column)
    new = tree([packed[j] * wide8(top[j : j + 1, :]) for j in range(8)])
    for j in range(8):
        new = jnp.where(lane == at + j, packed[j], new)
    rows = [wide8(new[j : j + 1, :]) for j in range(8)]
    inside = (lane >= at) & (lane < at + 8)
    out = []
    for t, tile in enumerate(tiles):
        if t == at // 8:
            out.append(new)
        else:
            change = tree([wide8(tile[:, at + j : at + j + 1]) * rows[j] for j in range(8)])
            out.append(jnp.where(inside, 0.0, tile) - change)
    return out


def inverse128(a, beside):
    def quarter(q, a):
        beside(q)
        tiles = [a[8 * t : 8 * t + 8] for t in range(16)]
        for k in range(4):
            tiles = eight_pivots(tiles, 8 * k)
        return pltpu.roll(jnp.concatenate(tiles[4:] + tiles[:4], axis=0), 96, 1)

    return lax.fori_loop(0, 4, quarter, a)


def block_at(k):
    return pl.ds(pl.multiple_of(k * 128, 128), 128)


def invert(matrix, strip, column, after_step, after_band):
    def update(q):
        rows = block_at(q)
        matrix[rows, :] = matrix[rows, :] - dot(column[rows, :], strip[...], NN, HIGHEST)

    def step(k, diagonal):
        at, following = block_at(k), block_at(lax.rem(k + 1, 4))
        block = inverse128(diagonal, update)
        strip[...] = dot(block, matrix[at, :], NN, HIGHEST)
        strip[:, at] = block
        column[...] = matrix[:, at]
        column[at, :] = jnp.zeros((128, 128), F32)
        matrix[:, at] = jnp.zeros((FEATS, 128), F32)
        matrix[at, :] = strip[...]
        after_step(k)
        return matrix[following, following] - dot(
            column[following, :], strip[:, following], NN, HIGHEST
        )

    strip[...] = jnp.zeros_like(strip)
    column[...] = jnp.zeros_like(column)
    lax.fori_loop(0, 4, step, matrix[block_at(0), block_at(0)])
    for q in range(4):
        update(q)
        after_band(q)


def fit_kernel(
    mask, proj, phases, frames_hbm, targets_hbm,
    solved_hbm, fh_hbm, fl_hbm,
    fh, fl, frames, frames_high, frames_low, proj_high, proj_low, targets, kept, kept_came, blocks, gram, gram_came, gram_sum, damped, inverses, mixed, strip, column,
    cross, cross_came, own,
    b1, b2, b3, b4, b5, b6, b7, b8, b9, g1, g2, g3, g4, g5, g6, g7, g8, g9, c1, c2, c3, c4, c5, c6, c7, c8, c9,
    bs, br, bgs, bgr, gs, gr, ggs, ggr, cs, cr, cgs, cgr, pair_send, pair_recv, fwd_send, fwd_recv, deep_send, deep_recv, local,
):
    pos = position()
    core = pos["c"]
    twin = moved(pos, "c", 1)
    spot = (pos["x"], pos["y"], pos["z"])
    sent = []

    def pair(i, src, dst):
        return remote(src, dst, pair_send.at[i], pair_recv.at[i], twin)

    met = greet(pos)
    load_frames = pltpu.make_async_copy(frames_hbm, frames, local.at[2])
    load_frames.start()
    load = pltpu.make_async_copy(targets_hbm, targets, local.at[0])
    load.start()

    for s in range(STEPS):
        here = mask[s, 0:1, :] > 0.5
        kept[s, 0:3] = jnp.where(here, proj[0:384, :], 0.0).reshape(3, 4, 4, 8, FEATS)
        kept[s, 3, 0] = jnp.where(here, proj[384:416, :], 0.0).reshape(4, 8, FEATS)
        kept[s, 3, 1, 0:3] = jnp.where(here, proj[416:440, :], 0.0).reshape(3, 8, FEATS)
        kept[s, 3, 1, 3] = jnp.broadcast_to(jnp.where(here, phases[...], 0.0), (8, FEATS))
        kept[s, 3, 2:4] = jnp.zeros((2, 4, 8, FEATS), F32)
    met()
    thirds = ((0, 128), (128, 128), (256, 256))
    landing = ((b1, b2, b3), (b4, b5, b6), (b7, b8, b9))
    swap = pair(0, kept.at[1 - core], kept_came)
    swap.start()
    sent.append(swap)
    load_frames.wait()

    @pl.loop(0, 4)
    def _(i):
        at = pl.ds(pl.multiple_of(i * 256, 256), 256)
        high, low = halves(frames[:, at])
        frames_high[:, at] = high
        frames_low[:, at] = low

    swap.wait_recv()
    kept[core] = kept[core] + kept_came[...]
    part = kept.at[core]
    for stage in range(3):
        scatter_start(pos, part, thirds, landing, (bs, br), stage)
        sent += scatter_copies(pos, part, thirds, landing, (bs, br), stage)
        scatter_finish(pos, part, thirds, landing, (bs, br), stage)
    blocks[(core,) + spot] = kept[(core,) + spot]
    for stage in range(3):
        copies = gather_copies(pos, blocks.at[core], thirds, (bgs, bgr), stage)
        run_copies(copies)
        sent += copies
    swap = pair(1, blocks.at[core], blocks.at[core])
    swap.start()
    sent.append(swap)

    def features(s):
        high, low = halves(blocks[s].reshape(512, FEATS)[:440])
        proj_high[...] = high
        proj_low[...] = low
        lanes = pl.ds(pl.multiple_of(s * FEATS, FEATS), FEATS)

        for i in range(4):
            rows = slice(i * 256, i * 256 + 256)
            inner = dot3(
                (frames_high[:, rows], frames_low[:, rows]), (proj_high[...], proj_low[...]), TN
            )
            high, low = halves(scaled_cosine(inner + blocks[s, 3, 1, 3, 0:1, :]))
            fh[rows, lanes] = high
            fl[rows, lanes] = low

    features(core)
    swap.wait_recv()
    features(1 - core)
    stores = [
        pltpu.make_async_copy(fh, fh_hbm, local.at[3]),
        pltpu.make_async_copy(fl, fl_hbm, local.at[4]),
    ]
    for store in stores:
        store.start()

    def feats(start, n):
        at = pl.ds(pl.multiple_of(start, 256), n)
        return fh[:, at], fl[:, at]

    def gram_half(c):
        @pl.loop(0, 2)
        def _(i):
            rows = pl.ds(i * 2, 2)
            square = dot3(feats(c * 512 + i * 256, 256), feats(c * 512, 512), TN)
            gram[c, rows, :, :, :, 0:512] = square.reshape(2, 4, 4, 8, 512)
            mixed = dot3(feats(512 + i * 256, 256), feats(c * 256, 256), TN)
            gram[c, rows, :, :, :, 512:768] = mixed.reshape(2, 4, 4, 8, 256)

    def cross_rows(c, lo, hi):
        @pl.loop(lo, hi)
        def _(i):
            at = pl.ds(pl.multiple_of(c * 1024 + i * 256, 256), 256)
            rows = dot3(halves(targets[:, at]), (fh[...], fl[...]), TN)
            cross[c, i] = rows.reshape(4, 4, 16, 1024)

    gram_half(1 - core)
    gram_swap = pair(2, gram.at[1 - core], gram_came)
    gram_swap.start()
    gram_half(core)
    load.wait()
    gram_swap.wait_recv()
    gram[core] = gram[core] + gram_came[...]
    part = gram.at[core]
    thirds = ((0, 256), (256, 256), (512, 256))
    landing = ((g1, g2, g3), (g4, g5, g6), (g7, g8, g9))
    args = (pos, part, thirds, landing, (gs, gr))
    scatter_start(*args, 0)
    cross_rows(1 - core, 0, 4)
    cross_swap = pair(3, cross.at[1 - core], cross_came)
    cross_swap.start()
    scatter_finish(*args, 0)
    scatter_start(*args, 1)
    cross_rows(core, 0, 2)
    scatter_finish(*args, 1)
    scatter_start(*args, 2)
    cross_rows(core, 2, 4)
    scatter_finish(*args, 2)
    for stage in range(3):
        sent += scatter_copies(*args, stage)
    gram_sum[spot] = gram[(core,) + spot]
    for stage in range(3):
        copies = gather_copies(pos, gram_sum, thirds, (ggs, ggr), stage)
        for copy in copies:
            copy.start()
        if stage == 0:
            cross_swap.wait_recv()

            @pl.loop(0, 4)
            def _(i):
                cross[core, i] = cross[core, i] + cross_came[i]

        for copy in copies:
            copy.wait_recv()
        sent += copies
    sent += [gram_swap, cross_swap]

    part = cross.at[core]
    thirds = ((0, 384), (384, 384), (768, 256))
    landing = ((c1, c2, c3), (c4, c5, c6), (c7, c8, c9))
    args = (pos, part, thirds, landing, (cs, cr))
    scatter_start(*args, 0)
    mixed[core] = gram_sum[:, :, :, :, 512:768].reshape(512, 256)
    mixed_swap = pair(4, mixed.at[core], mixed.at[core])
    mixed_swap.start()
    square = gram_sum[:, :, :, :, 0:512].reshape(512, 512)
    eye = lax.broadcasted_iota(jnp.int32, square.shape, 0) == lax.broadcasted_iota(jnp.int32, square.shape, 1)
    trace = jnp.sum(jnp.where(eye, square, 0.0), keepdims=True)
    square = jnp.where(eye, square + trace * (0.1 / FEATS), square)
    damped[core] = square
    damped_swap = pair(5, damped.at[core], damped.at[core])
    damped_swap.start()
    matrix = inverses.at[core]
    matrix[...] = square

    def after_step(k):
        @pl.when(k == 1)
        def _():
            scatter_finish(*args, 0)
            scatter_start(*args, 1)

        @pl.when(k == 2)
        def _():
            scatter_finish(*args, 1)
            scatter_start(*args, 2)

    swaps = []

    def after_band(q):
        band = matrix.at[pl.ds(q * 128, 128)]
        swap = remote(band, band, fwd_send.at[3, q], fwd_recv.at[3, q], twin)
        swap.start()
        swaps.append(swap)

    invert(matrix, strip, column, after_step, after_band)

    scatter_finish(*args, 2)
    for stage in range(3):
        sent += scatter_copies(*args, stage)
    sent += [mixed_swap, damped_swap] + swaps

    mixed_swap.wait_recv()
    damped_swap.wait_recv()
    for swap in swaps:
        swap.wait_recv()
    mine = cross[(core,) + spot]

    def solve(step, right):
        inverse = halves(inverses[step])
        guess = dot3(halves(right), inverse, NN)
        left_over = right - dot(guess, damped[step], NN, HIGHEST)
        return guess + dot3(halves(left_over), inverse, NN)

    w0 = solve(0, mine[:, :FEATS])
    seen = dot(w0[:, :256], mixed[0], NT, HIGHEST) + dot(w0[:, 256:], mixed[1], NT, HIGHEST)
    w1 = solve(1, mine[:, FEATS:] - seen)
    own[:, :FEATS] = w0
    own[:, FEATS:] = w1

    whole = solved_hbm.at[core]
    keep = pltpu.make_async_copy(own, whole.at[spot], local.at[1])
    keep.start()
    copies = gather_copies(pos, whole, thirds, (cgs, cgr), 0, own)
    run_copies(copies)
    keep.wait()
    sent += copies
    copies = gather_copies(pos, whole, thirds, (cgs, cgr), 1)
    for copy in copies:
        copy.start()
    sent += copies

    deep = {}
    for d in (0, 1, 3, 2):
        for color, order in enumerate(ORDERS):
            lo, n = thirds[color]
            origin = pos
            if d:
                copies[3 * color + d - 1].wait_recv()
                origin = moved(pos, order[1], 4 - d)
            at = region(origin, order[:2]) + (slice(None), pl.ds(lo, n))
            for e in (1, 2, 3):
                copy = remote(
                    whole.at[at], whole.at[at],
                    deep_send.at[color, d, e - 1], deep_recv.at[color, d, e - 1],
                    moved(pos, order[0], e),
                )
                copy.start()
                deep[color, d, e] = copy
                sent.append(copy)

    forwarded = []
    for e in (0, 1, 3, 2):
        for color, order in enumerate(ORDERS):
            lo, n = thirds[color]
            origin = pos
            if e:
                for d in range(4):
                    deep[color, d, e].wait_recv()
                origin = moved(pos, order[0], 4 - e)
            at = region(origin, order[:1]) + (slice(None), pl.ds(lo, n))
            copy = remote(whole.at[at], whole.at[at], fwd_send.at[color, e], fwd_recv.at[color, e], twin)
            copy.start()
            forwarded.append(copy)
    for copy in forwarded:
        copy.wait_recv()
    sent += forwarded
    for store in stores:
        store.wait()
    for copy in sent:
        copy.wait_send()


def landings(rows, widths):
    return [
        *[pltpu.VMEM((3, 4, 4, rows, n), F32) for n in widths],
        *[pltpu.VMEM((3, 4, rows, n), F32) for n in widths],
        *[pltpu.VMEM((3, rows, n), F32) for n in widths],
    ]


IN_VMEM = pl.BlockSpec(memory_space=pltpu.VMEM)
IN_HBM = pl.BlockSpec(memory_space=pl.ANY)


def fit(mask, proj, phases, frames, targets):
    return pl.pallas_call(
        fit_kernel,
        out_shape=(
            jax.ShapeDtypeStruct((2, 4, 4, 4, 16, 1024), F32),
            jax.ShapeDtypeStruct((1024, 1024), BF16),
            jax.ShapeDtypeStruct((1024, 1024), BF16),
        ),
        in_specs=[IN_VMEM, IN_VMEM, IN_VMEM, IN_HBM, IN_HBM],
        out_specs=(IN_HBM, IN_HBM, IN_HBM),
        scratch_shapes=[
            pltpu.VMEM((1024, 1024), BF16),
            pltpu.VMEM((1024, 1024), BF16),
            pltpu.VMEM((440, 1024), F32),
            pltpu.VMEM((440, 1024), BF16),
            pltpu.VMEM((440, 1024), BF16),
            pltpu.VMEM((440, FEATS), BF16),
            pltpu.VMEM((440, FEATS), BF16),
            pltpu.VMEM((1024, 2048), F32),
            pltpu.VMEM((2, 4, 4, 4, 8, FEATS), F32),
            pltpu.VMEM((4, 4, 4, 8, FEATS), F32),
            pltpu.VMEM((2, 4, 4, 4, 8, FEATS), F32),
            pltpu.VMEM((2, 4, 4, 4, 8, 768), F32),
            pltpu.VMEM((4, 4, 4, 8, 768), F32),
            pltpu.VMEM((4, 4, 4, 8, 768), F32),
            pltpu.VMEM((STEPS, FEATS, FEATS), F32),
            pltpu.VMEM((STEPS, FEATS, FEATS), F32),
            pltpu.VMEM((2, FEATS, 256), F32),
            pltpu.VMEM((128, FEATS), F32),
            pltpu.VMEM((FEATS, 128), F32),
            pltpu.VMEM((2, 4, 4, 4, 16, 1024), F32),
            pltpu.VMEM((4, 4, 4, 16, 1024), F32),
            pltpu.VMEM((16, 1024), F32),
            *landings(8, (128, 128, 256)),
            *landings(8, (256, 256, 256)),
            *landings(16, (384, 384, 256)),
            *[pltpu.SemaphoreType.DMA((3, 3, 3)) for _ in range(12)],
            pltpu.SemaphoreType.DMA((6,)),
            pltpu.SemaphoreType.DMA((6,)),
            pltpu.SemaphoreType.DMA((4, 4)),
            pltpu.SemaphoreType.DMA((4, 4)),
            pltpu.SemaphoreType.DMA((3, 4, 3)),
            pltpu.SemaphoreType.DMA((3, 4, 3)),
            pltpu.SemaphoreType.DMA((5,)),
        ],
        compiler_params=pltpu.CompilerParams(
            collective_id=1, has_side_effects=True, vmem_limit_bytes=60 << 20
        ),
    )(mask, proj, phases, frames, targets)


def residual_kernel(targets, solved, fh, fl, residual, weights):
    rows = solved[...]
    residual[...] = targets[...] - dot3((fh[...], fl[...]), halves(rows), NT)
    for s in range(STEPS):
        weights[s] = rows[:, s * FEATS : (s + 1) * FEATS].T


def residual_of(targets, solved, fh, fl):
    n = 256
    return pl.pallas_call(
        residual_kernel,
        grid=(2048 // n,),
        out_shape=(
            jax.ShapeDtypeStruct((1024, 2048), F32),
            jax.ShapeDtypeStruct((STEPS, FEATS, 2048), F32),
        ),
        in_specs=[
            pl.BlockSpec((1024, n), lambda i: (0, i)),
            pl.BlockSpec((n, 1024), lambda i: (i, 0)),
            IN_VMEM,
            IN_VMEM,
        ],
        out_specs=(
            pl.BlockSpec((1024, n), lambda i: (0, i)),
            pl.BlockSpec((STEPS, FEATS, n), lambda i: (0, 0, i)),
        ),
        compiler_params=pltpu.CompilerParams(vmem_limit_bytes=60 << 20),
    )(targets, solved, fh, fl)


def per_device(frames, targets, projection, phases, block_order):
    me = lax.axis_index("wide") * 4 + lax.axis_index("narrow")
    mask = (block_order[:STEPS] == me).astype(F32)
    mask = jnp.broadcast_to(mask[:, None, None], (STEPS, 8, FEATS))
    solved, fh, fl = fit(mask, projection[0], phases, frames.T, targets)
    return residual_of(targets, solved.reshape(2048, 1024), fh, fl)


def solution(mesh):
    return jax.shard_map(
        per_device,
        mesh=mesh,
        in_specs=(
            P(("wide", "narrow"), None),
            P(("wide", "narrow"), None),
            P(("wide", "narrow"), None, None),
            P(("wide", "narrow"), None),
            P(),
        ),
        out_specs=(P(("wide", "narrow"), None), P()),
        check_vma=False,
    )
```

```python
import jax
import jax.numpy as jnp
from jax import lax
from jax.experimental import pallas as pl
from jax.experimental.pallas import tpu as pltpu
from jax.sharding import PartitionSpec as P

STEPS = 2
FEATS = 512
MESH = pl.DeviceIdType.MESH
AXES = "xyz"
ORDERS = ("xyz", "yzx", "zxy")
HIGHEST = lax.Precision.HIGHEST
BF16 = jnp.bfloat16
F32 = jnp.float32
TN, NN, NT = ((0,), (0,)), ((1,), (0,)), ((1,), (1,))


def position():
    wide = lax.axis_index("wide")
    return {
        "x": lax.axis_index("narrow"),
        "y": lax.rem(lax.div(wide, 2), 4),
        "z": lax.div(wide, 8),
        "c": lax.rem(wide, 2),
    }


def device_of(pos):
    return ((pos["z"] * 4 + pos["y"]) * 2 + pos["c"], pos["x"])


def moved(pos, axis, step):
    new = dict(pos)
    if axis == "c":
        new["c"] = 1 - pos["c"]
    else:
        new[axis] = lax.rem(pos[axis] + step, 4)
    return new


def greet(pos):
    barrier = pltpu.get_barrier_semaphore()
    peers = [moved(pos, "c", 1)] + [moved(pos, a, d) for a in AXES for d in (1, 2, 3)]
    for peer in peers:
        pl.semaphore_signal(barrier, inc=1, device_id=device_of(peer), device_id_type=MESH)
    return lambda: pl.semaphore_wait(barrier, len(peers))


def region(pos, fixed):
    return tuple(pos[a] if a in fixed else slice(None) for a in AXES)


def remote(src, dst, send, recv, peer):
    return pltpu.make_async_remote_copy(
        src_ref=src, dst_ref=dst, send_sem=send, recv_sem=recv,
        device_id=device_of(peer), device_id_type=MESH,
    )


def scatter_copies(pos, part, lanes, landing, sems, stage):
    send, recv = sems
    copies = []
    for color, order in enumerate(ORDERS):
        lo, n = lanes[color]
        for d in (1, 2, 3):
            peer = moved(pos, order[stage], d)
            src = part.at[region(peer, order[: stage + 1]) + (slice(None), pl.ds(lo, n))]
            copies.append(remote(
                src, landing[stage][color].at[d - 1],
                send.at[stage, color, d - 1], recv.at[stage, color, d - 1], peer,
            ))
    return copies


def scatter_start(*args):
    for copy in scatter_copies(*args):
        copy.start()


def scatter_finish(pos, part, lanes, landing, sems, stage):
    copies = scatter_copies(pos, part, lanes, landing, sems, stage)
    for color, order in enumerate(ORDERS):
        lo, n = lanes[color]
        for copy in copies[3 * color : 3 * color + 3]:
            copy.wait_recv()
        at = region(pos, order[: stage + 1]) + (slice(None), pl.ds(lo, n))
        came = landing[stage][color]
        part[at] = part[at] + came[0] + came[1] + came[2]


def gather_copies(pos, whole, lanes, sems, stage, own=None):
    send, recv = sems
    copies = []
    for color, order in enumerate(ORDERS):
        lo, n = lanes[color]
        at = region(pos, order[: 3 - stage]) + (slice(None), pl.ds(lo, n))
        src = whole.at[at] if own is None else own.at[:, pl.ds(lo, n)]
        for d in (1, 2, 3):
            copies.append(remote(
                src, whole.at[at],
                send.at[stage, color, d - 1], recv.at[stage, color, d - 1],
                moved(pos, order[2 - stage], d),
            ))
    return copies


def run_copies(copies):
    for copy in copies:
        copy.start()
    for copy in copies:
        copy.wait_recv()


def halves(x):
    high = x.astype(BF16)
    return high, (x - high.astype(F32)).astype(BF16)


def dot(left, right, dims=NN, precision=None):
    return lax.dot_general(
        left, right, (dims, ((), ())), precision=precision, preferred_element_type=F32
    )


def dot3(left, right, dims):
    (lh, ll), (rh, rl) = left, right
    return dot(lh, rh, dims) + dot(lh, rl, dims) + dot(ll, rh, dims)


def scaled_cosine(angle):
    turns = jnp.round(angle * 0.15915494309189535)
    half = (angle * 0.5 - turns * 3.140625) - turns * 9.67653589793e-4
    z = half * half
    poly = -2.50521083854e-8
    for coef in (2.75573192239e-6, -1.98412698413e-4, 8.33333333333e-3, -1.66666666667e-1):
        poly = poly * z + coef
    sine = half + half * (z * poly)
    return 0.0625 - 0.125 * (sine * sine)


def wide8(x):
    return jnp.broadcast_to(x, (8, 128))


def tree(terms):
    while len(terms) > 1:
        terms = [a + b for a, b in zip(terms[::2], terms[1::2])]
    return terms[0]


def eight_pivots(tiles, at):
    lane = lax.broadcasted_iota(jnp.int32, (8, 128), 1)
    row = lax.broadcasted_iota(jnp.int32, (8, 128), 0)
    top = tiles[at // 8]
    columns = [wide8(top[:, at + j : at + j + 1]) for j in range(8)]
    d = [[wide8(columns[j][i : i + 1, :]) for j in range(8)] for i in range(8)]
    for p in range(8):
        inv = 1.0 / d[p][p]
        scaled = [inv if j == p else d[p][j] * inv for j in range(8)]
        for i in range(8):
            if i != p:
                c = d[i][p]
                d[i] = [-c * inv if j == p else d[i][j] - c * scaled[j] for j in range(8)]
        d[p] = scaled
    packed = []
    for j in range(8):
        column = d[0][j]
        for i in range(1, 8):
            column = jnp.where(row == i, d[i][j], column)
        packed.append(column)
    new = tree([packed[j] * wide8(top[j : j + 1, :]) for j in range(8)])
    for j in range(8):
        new = jnp.where(lane == at + j, packed[j], new)
    rows = [wide8(new[j : j + 1, :]) for j in range(8)]
    inside = (lane >= at) & (lane < at + 8)
    out = []
    for t, tile in enumerate(tiles):
        if t == at // 8:
            out.append(new)
        else:
            change = tree([wide8(tile[:, at + j : at + j + 1]) * rows[j] for j in range(8)])
            out.append(jnp.where(inside, 0.0, tile) - change)
    return out


def inverse128(a, beside):
    def quarter(q, a):
        beside(q)
        tiles = [a[8 * t : 8 * t + 8] for t in range(16)]
        for k in range(4):
            tiles = eight_pivots(tiles, 8 * k)
        return pltpu.roll(jnp.concatenate(tiles[4:] + tiles[:4], axis=0), 96, 1)

    return lax.fori_loop(0, 4, quarter, a)


def block_at(k):
    return pl.ds(pl.multiple_of(k * 128, 128), 128)


def invert(matrix, strip, column, after_step, after_band):
    def update(q):
        rows = block_at(q)
        matrix[rows, :] = matrix[rows, :] - dot(column[rows, :], strip[...], NN, HIGHEST)

    def step(k, diagonal):
        at, following = block_at(k), block_at(lax.rem(k + 1, 4))
        block = inverse128(diagonal, update)
        strip[...] = dot(block, matrix[at, :], NN, HIGHEST)
        strip[:, at] = block
        column[...] = matrix[:, at]
        column[at, :] = jnp.zeros((128, 128), F32)
        matrix[:, at] = jnp.zeros((FEATS, 128), F32)
        matrix[at, :] = strip[...]
        after_step(k)
        return matrix[following, following] - dot(
            column[following, :], strip[:, following], NN, HIGHEST
        )

    strip[...] = jnp.zeros_like(strip)
    column[...] = jnp.zeros_like(column)
    lax.fori_loop(0, 4, step, matrix[block_at(0), block_at(0)])
    for q in range(4):
        update(q)
        after_band(q)


def fit_kernel(
    visited, phases, proj_hbm, frames_hbm, targets_hbm,
    solved_hbm, fh_hbm, fl_hbm,
    fh, fl, proj, frames, frames_high, frames_low, proj_high, proj_low, targets, kept, kept_came, blocks, gram, gram_came, gram_sum, damped, inverses, mixed, strip, column,
    cross, cross_came, own,
    b1, b2, b3, b4, b5, b6, b7, b8, b9, g1, g2, g3, g4, g5, g6, g7, g8, g9, c1, c2, c3, c4, c5, c6, c7, c8, c9,
    bs, br, bgs, bgr, gs, gr, ggs, ggr, cs, cr, cgs, cgr, pair_send, pair_recv, fwd_send, fwd_recv, deep_send, deep_recv, local,
):
    pos = position()
    core = pos["c"]
    twin = moved(pos, "c", 1)
    spot = (pos["x"], pos["y"], pos["z"])
    sent = []

    def pair(i, src, dst):
        return remote(src, dst, pair_send.at[i], pair_recv.at[i], twin)

    met = greet(pos)
    load_proj = pltpu.make_async_copy(proj_hbm, proj, local.at[5])
    load_proj.start()
    load_frames = pltpu.make_async_copy(frames_hbm, frames, local.at[2])
    load_frames.start()
    load = pltpu.make_async_copy(targets_hbm, targets, local.at[0])
    load.start()

    me = lax.axis_index("wide") * 4 + lax.axis_index("narrow")
    load_proj.wait()
    for s in range(STEPS):
        here = jnp.full((1, FEATS), visited[s], jnp.int32) == me
        kept[s, 0:3] = jnp.where(here, proj[0:384, :], 0.0).reshape(3, 4, 4, 8, FEATS)
        kept[s, 3, 0] = jnp.where(here, proj[384:416, :], 0.0).reshape(4, 8, FEATS)
        kept[s, 3, 1, 0:3] = jnp.where(here, proj[416:440, :], 0.0).reshape(3, 8, FEATS)
        kept[s, 3, 1, 3] = jnp.broadcast_to(jnp.where(here, phases[...], 0.0), (8, FEATS))
        kept[s, 3, 2:4] = jnp.zeros((2, 4, 8, FEATS), F32)
    met()
    thirds = ((0, 128), (128, 128), (256, 256))
    landing = ((b1, b2, b3), (b4, b5, b6), (b7, b8, b9))
    swap = pair(0, kept.at[1 - core], kept_came)
    swap.start()
    sent.append(swap)
    load_frames.wait()

    @pl.loop(0, 4)
    def _(i):
        at = pl.ds(pl.multiple_of(i * 256, 256), 256)
        high, low = halves(frames[:, at])
        frames_high[:, at] = high
        frames_low[:, at] = low

    swap.wait_recv()
    kept[core] = kept[core] + kept_came[...]
    part = kept.at[core]
    for stage in range(3):
        scatter_start(pos, part, thirds, landing, (bs, br), stage)
        sent += scatter_copies(pos, part, thirds, landing, (bs, br), stage)
        scatter_finish(pos, part, thirds, landing, (bs, br), stage)
    blocks[(core,) + spot] = kept[(core,) + spot]
    for stage in range(3):
        copies = gather_copies(pos, blocks.at[core], thirds, (bgs, bgr), stage)
        run_copies(copies)
        sent += copies
    swap = pair(1, blocks.at[core], blocks.at[core])
    swap.start()
    sent.append(swap)

    def features(s):
        high, low = halves(blocks[s].reshape(512, FEATS)[:440])
        proj_high[...] = high
        proj_low[...] = low
        lanes = pl.ds(pl.multiple_of(s * FEATS, FEATS), FEATS)

        for i in range(4):
            rows = slice(i * 256, i * 256 + 256)
            inner = dot3(
                (frames_high[:, rows], frames_low[:, rows]), (proj_high[...], proj_low[...]), TN
            )
            high, low = halves(scaled_cosine(inner + blocks[s, 3, 1, 3, 0:1, :]))
            fh[rows, lanes] = high
            fl[rows, lanes] = low

    features(core)
    swap.wait_recv()
    features(1 - core)
    stores = [
        pltpu.make_async_copy(fh, fh_hbm, local.at[3]),
        pltpu.make_async_copy(fl, fl_hbm, local.at[4]),
    ]
    for store in stores:
        store.start()

    def feats(start, n):
        at = pl.ds(pl.multiple_of(start, 256), n)
        return fh[:, at], fl[:, at]

    def gram_half(c):
        @pl.loop(0, 2)
        def _(i):
            rows = pl.ds(i * 2, 2)
            square = dot3(feats(c * 512 + i * 256, 256), feats(c * 512, 512), TN)
            gram[c, rows, :, :, :, 0:512] = square.reshape(2, 4, 4, 8, 512)
            mixed = dot3(feats(512 + i * 256, 256), feats(c * 256, 256), TN)
            gram[c, rows, :, :, :, 512:768] = mixed.reshape(2, 4, 4, 8, 256)

    def cross_rows(c, lo, hi):
        @pl.loop(lo, hi)
        def _(i):
            at = pl.ds(pl.multiple_of(c * 1024 + i * 256, 256), 256)
            rows = dot3(halves(targets[:, at]), (fh[...], fl[...]), TN)
            cross[c, i] = rows.reshape(4, 4, 16, 1024)

    gram_half(1 - core)
    gram_swap = pair(2, gram.at[1 - core], gram_came)
    gram_swap.start()
    gram_half(core)
    load.wait()
    gram_swap.wait_recv()
    gram[core] = gram[core] + gram_came[...]
    part = gram.at[core]
    thirds = ((0, 256), (256, 256), (512, 256))
    landing = ((g1, g2, g3), (g4, g5, g6), (g7, g8, g9))
    args = (pos, part, thirds, landing, (gs, gr))
    scatter_start(*args, 0)
    cross_rows(1 - core, 0, 4)
    cross_swap = pair(3, cross.at[1 - core], cross_came)
    cross_swap.start()
    scatter_finish(*args, 0)
    scatter_start(*args, 1)
    cross_rows(core, 0, 2)
    scatter_finish(*args, 1)
    scatter_start(*args, 2)
    cross_rows(core, 2, 4)
    scatter_finish(*args, 2)
    for stage in range(3):
        sent += scatter_copies(*args, stage)
    gram_sum[spot] = gram[(core,) + spot]
    for stage in range(3):
        copies = gather_copies(pos, gram_sum, thirds, (ggs, ggr), stage)
        for copy in copies:
            copy.start()
        if stage == 0:
            cross_swap.wait_recv()

            @pl.loop(0, 4)
            def _(i):
                cross[core, i] = cross[core, i] + cross_came[i]

        for copy in copies:
            copy.wait_recv()
        sent += copies
    sent += [gram_swap, cross_swap]

    part = cross.at[core]
    thirds = ((0, 384), (384, 384), (768, 256))
    landing = ((c1, c2, c3), (c4, c5, c6), (c7, c8, c9))
    args = (pos, part, thirds, landing, (cs, cr))
    scatter_start(*args, 0)
    mixed[core] = gram_sum[:, :, :, :, 512:768].reshape(512, 256)
    mixed_swap = pair(4, mixed.at[core], mixed.at[core])
    mixed_swap.start()
    square = gram_sum[:, :, :, :, 0:512].reshape(512, 512)
    eye = lax.broadcasted_iota(jnp.int32, square.shape, 0) == lax.broadcasted_iota(jnp.int32, square.shape, 1)
    trace = jnp.sum(jnp.where(eye, square, 0.0), keepdims=True)
    square = jnp.where(eye, square + trace * (0.1 / FEATS), square)
    damped[core] = square
    damped_swap = pair(5, damped.at[core], damped.at[core])
    damped_swap.start()
    matrix = inverses.at[core]
    matrix[...] = square

    def after_step(k):
        @pl.when(k == 1)
        def _():
            scatter_finish(*args, 0)
            scatter_start(*args, 1)

        @pl.when(k == 2)
        def _():
            scatter_finish(*args, 1)
            scatter_start(*args, 2)

    swaps = []

    def after_band(q):
        band = matrix.at[pl.ds(q * 128, 128)]
        swap = remote(band, band, fwd_send.at[3, q], fwd_recv.at[3, q], twin)
        swap.start()
        swaps.append(swap)

    invert(matrix, strip, column, after_step, after_band)

    scatter_finish(*args, 2)
    for stage in range(3):
        sent += scatter_copies(*args, stage)
    sent += [mixed_swap, damped_swap] + swaps

    mixed_swap.wait_recv()
    damped_swap.wait_recv()
    for swap in swaps:
        swap.wait_recv()
    mine = cross[(core,) + spot]

    def solve(step, right):
        inverse = halves(inverses[step])
        guess = dot3(halves(right), inverse, NN)
        left_over = right - dot(guess, damped[step], NN, HIGHEST)
        return guess + dot3(halves(left_over), inverse, NN)

    w0 = solve(0, mine[:, :FEATS])
    seen = dot(w0[:, :256], mixed[0], NT, HIGHEST) + dot(w0[:, 256:], mixed[1], NT, HIGHEST)
    w1 = solve(1, mine[:, FEATS:] - seen)
    own[:, :FEATS] = w0
    own[:, FEATS:] = w1

    whole = solved_hbm.at[core]
    keep = pltpu.make_async_copy(own, whole.at[spot], local.at[1])
    keep.start()
    copies = gather_copies(pos, whole, thirds, (cgs, cgr), 0, own)
    run_copies(copies)
    keep.wait()
    sent += copies
    copies = gather_copies(pos, whole, thirds, (cgs, cgr), 1)
    for copy in copies:
        copy.start()
    sent += copies

    deep = {}
    for d in (0, 1, 3, 2):
        for color, order in enumerate(ORDERS):
            lo, n = thirds[color]
            origin = pos
            if d:
                copies[3 * color + d - 1].wait_recv()
                origin = moved(pos, order[1], 4 - d)
            at = region(origin, order[:2]) + (slice(None), pl.ds(lo, n))
            for e in (1, 2, 3):
                copy = remote(
                    whole.at[at], whole.at[at],
                    deep_send.at[color, d, e - 1], deep_recv.at[color, d, e - 1],
                    moved(pos, order[0], e),
                )
                copy.start()
                deep[color, d, e] = copy
                sent.append(copy)

    forwarded = []
    for e in (0, 1, 3, 2):
        for color, order in enumerate(ORDERS):
            lo, n = thirds[color]
            origin = pos
            if e:
                for d in range(4):
                    deep[color, d, e].wait_recv()
                origin = moved(pos, order[0], 4 - e)
            at = region(origin, order[:1]) + (slice(None), pl.ds(lo, n))
            copy = remote(whole.at[at], whole.at[at], fwd_send.at[color, e], fwd_recv.at[color, e], twin)
            copy.start()
            forwarded.append(copy)
    for copy in forwarded:
        copy.wait_recv()
    sent += forwarded
    for store in stores:
        store.wait()
    for copy in sent:
        copy.wait_send()


def landings(rows, widths):
    return [
        *[pltpu.VMEM((3, 4, 4, rows, n), F32) for n in widths],
        *[pltpu.VMEM((3, 4, rows, n), F32) for n in widths],
        *[pltpu.VMEM((3, rows, n), F32) for n in widths],
    ]


IN_VMEM = pl.BlockSpec(memory_space=pltpu.VMEM)
IN_HBM = pl.BlockSpec(memory_space=pl.ANY)


def fit(visited, phases, proj, frames, targets):
    return pl.pallas_call(
        fit_kernel,
        out_shape=(
            jax.ShapeDtypeStruct((2, 4, 4, 4, 16, 1024), F32),
            jax.ShapeDtypeStruct((1024, 1024), BF16),
            jax.ShapeDtypeStruct((1024, 1024), BF16),
        ),
        in_specs=[pl.BlockSpec(memory_space=pltpu.SMEM), IN_VMEM, IN_HBM, IN_HBM, IN_HBM],
        out_specs=(IN_HBM, IN_HBM, IN_HBM),
        scratch_shapes=[
            pltpu.VMEM((1024, 1024), BF16),
            pltpu.VMEM((1024, 1024), BF16),
            pltpu.VMEM((440, FEATS), F32),
            pltpu.VMEM((440, 1024), F32),
            pltpu.VMEM((440, 1024), BF16),
            pltpu.VMEM((440, 1024), BF16),
            pltpu.VMEM((440, FEATS), BF16),
            pltpu.VMEM((440, FEATS), BF16),
            pltpu.VMEM((1024, 2048), F32),
            pltpu.VMEM((2, 4, 4, 4, 8, FEATS), F32),
            pltpu.VMEM((4, 4, 4, 8, FEATS), F32),
            pltpu.VMEM((2, 4, 4, 4, 8, FEATS), F32),
            pltpu.VMEM((2, 4, 4, 4, 8, 768), F32),
            pltpu.VMEM((4, 4, 4, 8, 768), F32),
            pltpu.VMEM((4, 4, 4, 8, 768), F32),
            pltpu.VMEM((STEPS, FEATS, FEATS), F32),
            pltpu.VMEM((STEPS, FEATS, FEATS), F32),
            pltpu.VMEM((2, FEATS, 256), F32),
            pltpu.VMEM((128, FEATS), F32),
            pltpu.VMEM((FEATS, 128), F32),
            pltpu.VMEM((2, 4, 4, 4, 16, 1024), F32),
            pltpu.VMEM((4, 4, 4, 16, 1024), F32),
            pltpu.VMEM((16, 1024), F32),
            *landings(8, (128, 128, 256)),
            *landings(8, (256, 256, 256)),
            *landings(16, (384, 384, 256)),
            *[pltpu.SemaphoreType.DMA((3, 3, 3)) for _ in range(12)],
            pltpu.SemaphoreType.DMA((6,)),
            pltpu.SemaphoreType.DMA((6,)),
            pltpu.SemaphoreType.DMA((4, 4)),
            pltpu.SemaphoreType.DMA((4, 4)),
            pltpu.SemaphoreType.DMA((3, 4, 3)),
            pltpu.SemaphoreType.DMA((3, 4, 3)),
            pltpu.SemaphoreType.DMA((6,)),
        ],
        compiler_params=pltpu.CompilerParams(
            collective_id=1, has_side_effects=True, vmem_limit_bytes=60 << 20
        ),
    )(visited, phases, proj, frames, targets)


def residual_kernel(targets, solved, fh, fl, residual, weights):
    columns = [solved[:, s * FEATS : (s + 1) * FEATS].T for s in range(STEPS)]
    fitted = dot3((fh[...], fl[...]), halves(jnp.concatenate(columns, axis=0)), NN)
    residual[...] = targets[...] - fitted
    for s in range(STEPS):
        weights[s] = columns[s]


def residual_of(targets, solved, fh, fl):
    n = 512
    return pl.pallas_call(
        residual_kernel,
        grid=(2048 // n,),
        out_shape=(
            jax.ShapeDtypeStruct((1024, 2048), F32),
            jax.ShapeDtypeStruct((STEPS, FEATS, 2048), F32),
        ),
        in_specs=[
            pl.BlockSpec((1024, n), lambda i: (0, i)),
            pl.BlockSpec((n, 1024), lambda i: (i, 0)),
            IN_VMEM,
            IN_VMEM,
        ],
        out_specs=(
            pl.BlockSpec((1024, n), lambda i: (0, i)),
            pl.BlockSpec((STEPS, FEATS, n), lambda i: (0, 0, i)),
        ),
        compiler_params=pltpu.CompilerParams(vmem_limit_bytes=60 << 20),
    )(targets, solved, fh, fl)


def per_device(frames, targets, projection, phases, block_order):
    solved, fh, fl = fit(block_order, phases, projection[0], frames.T, targets)
    return residual_of(targets, solved.reshape(2048, 1024), fh, fl)


def solution(mesh):
    return jax.shard_map(
        per_device,
        mesh=mesh,
        in_specs=(
            P(("wide", "narrow"), None),
            P(("wide", "narrow"), None),
            P(("wide", "narrow"), None, None),
            P(("wide", "narrow"), None),
            P(),
        ),
        out_specs=(P(("wide", "narrow"), None), P()),
        check_vma=False,
    )
```

```python
import jax
import jax.numpy as jnp
from jax import lax
from jax.experimental import pallas as pl
from jax.experimental.pallas import tpu as pltpu
from jax.sharding import PartitionSpec as P

STEPS = 2
FEATS = 512
MESH = pl.DeviceIdType.MESH
AXES = "xyz"
ORDERS = ("xyz", "yzx", "zxy")
HIGHEST = lax.Precision.HIGHEST
BF16 = jnp.bfloat16
F32 = jnp.float32
TN, NN, NT = ((0,), (0,)), ((1,), (0,)), ((1,), (1,))


def position():
    wide = lax.axis_index("wide")
    return {
        "x": lax.axis_index("narrow"),
        "y": lax.rem(lax.div(wide, 2), 4),
        "z": lax.div(wide, 8),
        "c": lax.rem(wide, 2),
    }


def device_of(pos):
    return ((pos["z"] * 4 + pos["y"]) * 2 + pos["c"], pos["x"])


def moved(pos, axis, step):
    new = dict(pos)
    if axis == "c":
        new["c"] = 1 - pos["c"]
    else:
        new[axis] = lax.rem(pos[axis] + step, 4)
    return new


def greet(pos):
    barrier = pltpu.get_barrier_semaphore()
    peers = [moved(pos, "c", 1)] + [moved(pos, a, d) for a in AXES for d in (1, 2, 3)]
    for peer in peers:
        pl.semaphore_signal(barrier, inc=1, device_id=device_of(peer), device_id_type=MESH)
    return lambda: pl.semaphore_wait(barrier, len(peers))


def region(pos, fixed):
    return tuple(pos[a] if a in fixed else slice(None) for a in AXES)


def remote(src, dst, send, recv, peer):
    return pltpu.make_async_remote_copy(
        src_ref=src, dst_ref=dst, send_sem=send, recv_sem=recv,
        device_id=device_of(peer), device_id_type=MESH,
    )


def scatter_copies(pos, part, lanes, landing, sems, stage):
    send, recv = sems
    copies = []
    for color, order in enumerate(ORDERS):
        lo, n = lanes[color]
        for d in (1, 2, 3):
            peer = moved(pos, order[stage], d)
            src = part.at[region(peer, order[: stage + 1]) + (slice(None), pl.ds(lo, n))]
            copies.append(remote(
                src, landing[stage][color].at[d - 1],
                send.at[stage, color, d - 1], recv.at[stage, color, d - 1], peer,
            ))
    return copies


def scatter_start(*args):
    for copy in scatter_copies(*args):
        copy.start()


def scatter_finish(pos, part, lanes, landing, sems, stage):
    copies = scatter_copies(pos, part, lanes, landing, sems, stage)
    for color, order in enumerate(ORDERS):
        lo, n = lanes[color]
        for copy in copies[3 * color : 3 * color + 3]:
            copy.wait_recv()
        at = region(pos, order[: stage + 1]) + (slice(None), pl.ds(lo, n))
        came = landing[stage][color]
        part[at] = part[at] + came[0] + came[1] + came[2]


def gather_copies(pos, whole, lanes, sems, stage, own=None):
    send, recv = sems
    copies = []
    for color, order in enumerate(ORDERS):
        lo, n = lanes[color]
        at = region(pos, order[: 3 - stage]) + (slice(None), pl.ds(lo, n))
        src = whole.at[at] if own is None else own.at[:, pl.ds(lo, n)]
        for d in (1, 2, 3):
            copies.append(remote(
                src, whole.at[at],
                send.at[stage, color, d - 1], recv.at[stage, color, d - 1],
                moved(pos, order[2 - stage], d),
            ))
    return copies


def run_copies(copies):
    for copy in copies:
        copy.start()
    for copy in copies:
        copy.wait_recv()


def halves(x):
    high = x.astype(BF16)
    return high, (x - high.astype(F32)).astype(BF16)


def dot(left, right, dims=NN, precision=None):
    return lax.dot_general(
        left, right, (dims, ((), ())), precision=precision, preferred_element_type=F32
    )


def dot3(left, right, dims):
    (lh, ll), (rh, rl) = left, right
    return dot(lh, rh, dims) + dot(lh, rl, dims) + dot(ll, rh, dims)


def scaled_cosine(angle):
    turns = jnp.round(angle * 0.15915494309189535)
    half = (angle * 0.5 - turns * 3.140625) - turns * 9.67653589793e-4
    z = half * half
    poly = -2.50521083854e-8
    for coef in (2.75573192239e-6, -1.98412698413e-4, 8.33333333333e-3, -1.66666666667e-1):
        poly = poly * z + coef
    sine = half + half * (z * poly)
    return 0.0625 - 0.125 * (sine * sine)


def wide8(x):
    return jnp.broadcast_to(x, (8, 128))


def tree(terms):
    while len(terms) > 1:
        terms = [a + b for a, b in zip(terms[::2], terms[1::2])]
    return terms[0]


def eight_pivots(tiles, at):
    lane = lax.broadcasted_iota(jnp.int32, (8, 128), 1)
    row = lax.broadcasted_iota(jnp.int32, (8, 128), 0)
    top = tiles[at // 8]
    columns = [wide8(top[:, at + j : at + j + 1]) for j in range(8)]
    d = [[wide8(columns[j][i : i + 1, :]) for j in range(8)] for i in range(8)]
    for p in range(8):
        inv = 1.0 / d[p][p]
        scaled = [inv if j == p else d[p][j] * inv for j in range(8)]
        for i in range(8):
            if i != p:
                c = d[i][p]
                d[i] = [-c * inv if j == p else d[i][j] - c * scaled[j] for j in range(8)]
        d[p] = scaled
    packed = []
    for j in range(8):
        column = d[0][j]
        for i in range(1, 8):
            column = jnp.where(row == i, d[i][j], column)
        packed.append(column)
    new = tree([packed[j] * wide8(top[j : j + 1, :]) for j in range(8)])
    for j in range(8):
        new = jnp.where(lane == at + j, packed[j], new)
    rows = [wide8(new[j : j + 1, :]) for j in range(8)]
    inside = (lane >= at) & (lane < at + 8)
    out = []
    for t, tile in enumerate(tiles):
        if t == at // 8:
            out.append(new)
        else:
            change = tree([wide8(tile[:, at + j : at + j + 1]) * rows[j] for j in range(8)])
            out.append(jnp.where(inside, 0.0, tile) - change)
    return out


def inverse128(a, beside):
    def half(h, a):
        beside(2 * h)
        beside(2 * h + 1)
        tiles = [a[8 * t : 8 * t + 8] for t in range(16)]
        for k in range(8):
            tiles = eight_pivots(tiles, 8 * k)
        return pltpu.roll(jnp.concatenate(tiles[8:] + tiles[:8], axis=0), 64, 1)

    return lax.fori_loop(0, 2, half, a)


def block_at(k):
    return pl.ds(pl.multiple_of(k * 128, 128), 128)


def invert(matrix, strip, column, after_step, after_band):
    def update(q):
        rows = block_at(q)
        matrix[rows, :] = matrix[rows, :] - dot(column[rows, :], strip[...], NN, HIGHEST)

    def step(k, diagonal):
        at, following = block_at(k), block_at(lax.rem(k + 1, 4))
        block = inverse128(diagonal, update)
        strip[...] = dot(block, matrix[at, :], NN, HIGHEST)
        strip[:, at] = block
        column[...] = matrix[:, at]
        column[at, :] = jnp.zeros((128, 128), F32)
        matrix[:, at] = jnp.zeros((FEATS, 128), F32)
        matrix[at, :] = strip[...]
        after_step(k)
        return matrix[following, following] - dot(
            column[following, :], strip[:, following], NN, HIGHEST
        )

    strip[...] = jnp.zeros_like(strip)
    column[...] = jnp.zeros_like(column)
    lax.fori_loop(0, 4, step, matrix[block_at(0), block_at(0)])
    for q in range(4):
        update(q)
        after_band(q)


def fit_kernel(
    visited, phases, proj_hbm, frames_hbm, targets_hbm,
    solved_hbm, fh_hbm, fl_hbm,
    fh, fl, proj, frames, frames_high, frames_low, proj_high, proj_low, targets, kept, kept_came, blocks, gram, gram_came, gram_sum, damped, inverses, mixed, strip, column,
    cross, cross_came, own,
    b1, b2, b3, b4, b5, b6, b7, b8, b9, g1, g2, g3, g4, g5, g6, g7, g8, g9, c1, c2, c3, c4, c5, c6, c7, c8, c9,
    bs, br, bgs, bgr, gs, gr, ggs, ggr, cs, cr, cgs, cgr, pair_send, pair_recv, fwd_send, fwd_recv, deep_send, deep_recv, local,
):
    pos = position()
    core = pos["c"]
    twin = moved(pos, "c", 1)
    spot = (pos["x"], pos["y"], pos["z"])
    sent = []

    def pair(i, src, dst):
        return remote(src, dst, pair_send.at[i], pair_recv.at[i], twin)

    met = greet(pos)
    load_proj = pltpu.make_async_copy(proj_hbm, proj, local.at[5])
    load_proj.start()
    load_frames = pltpu.make_async_copy(frames_hbm, frames, local.at[2])
    load_frames.start()
    load = pltpu.make_async_copy(targets_hbm, targets, local.at[0])
    load.start()

    me = lax.axis_index("wide") * 4 + lax.axis_index("narrow")
    load_proj.wait()
    for s in range(STEPS):
        here = jnp.full((1, FEATS), visited[s], jnp.int32) == me
        kept[s, 0:3] = jnp.where(here, proj[0:384, :], 0.0).reshape(3, 4, 4, 8, FEATS)
        kept[s, 3, 0] = jnp.where(here, proj[384:416, :], 0.0).reshape(4, 8, FEATS)
        kept[s, 3, 1, 0:3] = jnp.where(here, proj[416:440, :], 0.0).reshape(3, 8, FEATS)
        kept[s, 3, 1, 3] = jnp.broadcast_to(jnp.where(here, phases[...], 0.0), (8, FEATS))
        kept[s, 3, 2:4] = jnp.zeros((2, 4, 8, FEATS), F32)
    met()
    thirds = ((0, 128), (128, 128), (256, 256))
    landing = ((b1, b2, b3), (b4, b5, b6), (b7, b8, b9))
    swap = pair(0, kept.at[1 - core], kept_came)
    swap.start()
    sent.append(swap)
    load_frames.wait()

    @pl.loop(0, 4)
    def _(i):
        at = pl.ds(pl.multiple_of(i * 256, 256), 256)
        high, low = halves(frames[:, at])
        frames_high[:, at] = high
        frames_low[:, at] = low

    swap.wait_recv()
    kept[core] = kept[core] + kept_came[...]
    part = kept.at[core]
    for stage in range(3):
        scatter_start(pos, part, thirds, landing, (bs, br), stage)
        sent += scatter_copies(pos, part, thirds, landing, (bs, br), stage)
        scatter_finish(pos, part, thirds, landing, (bs, br), stage)
    blocks[(core,) + spot] = kept[(core,) + spot]
    for stage in range(3):
        copies = gather_copies(pos, blocks.at[core], thirds, (bgs, bgr), stage)
        run_copies(copies)
        sent += copies
    swap = pair(1, blocks.at[core], blocks.at[core])
    swap.start()
    sent.append(swap)

    def features(s):
        high, low = halves(blocks[s].reshape(512, FEATS)[:440])
        proj_high[...] = high
        proj_low[...] = low
        lanes = pl.ds(pl.multiple_of(s * FEATS, FEATS), FEATS)

        for i in range(4):
            rows = slice(i * 256, i * 256 + 256)
            inner = dot3(
                (frames_high[:, rows], frames_low[:, rows]), (proj_high[...], proj_low[...]), TN
            )
            high, low = halves(scaled_cosine(inner + blocks[s, 3, 1, 3, 0:1, :]))
            fh[rows, lanes] = high
            fl[rows, lanes] = low

    features(core)
    swap.wait_recv()
    features(1 - core)
    stores = [
        pltpu.make_async_copy(fh, fh_hbm, local.at[3]),
        pltpu.make_async_copy(fl, fl_hbm, local.at[4]),
    ]
    for store in stores:
        store.start()

    def feats(start, n):
        at = pl.ds(pl.multiple_of(start, 256), n)
        return fh[:, at], fl[:, at]

    def gram_half(c):
        @pl.loop(0, 2)
        def _(i):
            rows = pl.ds(i * 2, 2)
            square = dot3(feats(c * 512 + i * 256, 256), feats(c * 512, 512), TN)
            gram[c, rows, :, :, :, 0:512] = square.reshape(2, 4, 4, 8, 512)
            mixed = dot3(feats(512 + i * 256, 256), feats(c * 256, 256), TN)
            gram[c, rows, :, :, :, 512:768] = mixed.reshape(2, 4, 4, 8, 256)

    def cross_rows(c, lo, hi):
        @pl.loop(lo, hi)
        def _(i):
            at = pl.ds(pl.multiple_of(c * 1024 + i * 256, 256), 256)
            rows = dot3(halves(targets[:, at]), (fh[...], fl[...]), TN)
            cross[c, i] = rows.reshape(4, 4, 16, 1024)

    gram_half(1 - core)
    gram_swap = pair(2, gram.at[1 - core], gram_came)
    gram_swap.start()
    gram_half(core)
    load.wait()
    gram_swap.wait_recv()
    gram[core] = gram[core] + gram_came[...]
    part = gram.at[core]
    thirds = ((0, 256), (256, 256), (512, 256))
    landing = ((g1, g2, g3), (g4, g5, g6), (g7, g8, g9))
    args = (pos, part, thirds, landing, (gs, gr))
    scatter_start(*args, 0)
    cross_rows(1 - core, 0, 4)
    cross_swap = pair(3, cross.at[1 - core], cross_came)
    cross_swap.start()
    scatter_finish(*args, 0)
    scatter_start(*args, 1)
    cross_rows(core, 0, 2)
    scatter_finish(*args, 1)
    scatter_start(*args, 2)
    cross_rows(core, 2, 4)
    scatter_finish(*args, 2)
    for stage in range(3):
        sent += scatter_copies(*args, stage)
    gram_sum[spot] = gram[(core,) + spot]
    for stage in range(3):
        copies = gather_copies(pos, gram_sum, thirds, (ggs, ggr), stage)
        for copy in copies:
            copy.start()
        if stage == 0:
            cross_swap.wait_recv()

            @pl.loop(0, 4)
            def _(i):
                cross[core, i] = cross[core, i] + cross_came[i]

        for copy in copies:
            copy.wait_recv()
        sent += copies
    sent += [gram_swap, cross_swap]

    part = cross.at[core]
    thirds = ((0, 384), (384, 384), (768, 256))
    landing = ((c1, c2, c3), (c4, c5, c6), (c7, c8, c9))
    args = (pos, part, thirds, landing, (cs, cr))
    scatter_start(*args, 0)
    mixed[core] = gram_sum[:, :, :, :, 512:768].reshape(512, 256)
    mixed_swap = pair(4, mixed.at[core], mixed.at[core])
    mixed_swap.start()
    square = gram_sum[:, :, :, :, 0:512].reshape(512, 512)
    eye = lax.broadcasted_iota(jnp.int32, square.shape, 0) == lax.broadcasted_iota(jnp.int32, square.shape, 1)
    trace = jnp.sum(jnp.where(eye, square, 0.0), keepdims=True)
    square = jnp.where(eye, square + trace * (0.1 / FEATS), square)
    damped[core] = square
    damped_swap = pair(5, damped.at[core], damped.at[core])
    damped_swap.start()
    matrix = inverses.at[core]
    matrix[...] = square

    def after_step(k):
        @pl.when(k == 1)
        def _():
            scatter_finish(*args, 0)
            scatter_start(*args, 1)

        @pl.when(k == 2)
        def _():
            scatter_finish(*args, 1)
            scatter_start(*args, 2)

    swaps = []

    def after_band(q):
        band = matrix.at[pl.ds(q * 128, 128)]
        swap = remote(band, band, fwd_send.at[3, q], fwd_recv.at[3, q], twin)
        swap.start()
        swaps.append(swap)

    invert(matrix, strip, column, after_step, after_band)

    scatter_finish(*args, 2)
    for stage in range(3):
        sent += scatter_copies(*args, stage)
    sent += [mixed_swap, damped_swap] + swaps

    mixed_swap.wait_recv()
    damped_swap.wait_recv()
    for swap in swaps:
        swap.wait_recv()
    mine = cross[(core,) + spot]

    def solve(step, right):
        inverse = halves(inverses[step])
        guess = dot3(halves(right), inverse, NN)
        left_over = right - dot(guess, damped[step], NN, HIGHEST)
        return guess + dot3(halves(left_over), inverse, NN)

    w0 = solve(0, mine[:, :FEATS])
    seen = dot(w0[:, :256], mixed[0], NT, HIGHEST) + dot(w0[:, 256:], mixed[1], NT, HIGHEST)
    w1 = solve(1, mine[:, FEATS:] - seen)
    own[:, :FEATS] = w0
    own[:, FEATS:] = w1

    whole = solved_hbm.at[core]
    keep = pltpu.make_async_copy(own, whole.at[spot], local.at[1])
    keep.start()
    copies = gather_copies(pos, whole, thirds, (cgs, cgr), 0, own)
    run_copies(copies)
    keep.wait()
    sent += copies
    copies = gather_copies(pos, whole, thirds, (cgs, cgr), 1)
    for copy in copies:
        copy.start()
    sent += copies

    deep = {}
    for d in (0, 1, 3, 2):
        for color, order in enumerate(ORDERS):
            lo, n = thirds[color]
            origin = pos
            if d:
                copies[3 * color + d - 1].wait_recv()
                origin = moved(pos, order[1], 4 - d)
            at = region(origin, order[:2]) + (slice(None), pl.ds(lo, n))
            for e in (1, 2, 3):
                copy = remote(
                    whole.at[at], whole.at[at],
                    deep_send.at[color, d, e - 1], deep_recv.at[color, d, e - 1],
                    moved(pos, order[0], e),
                )
                copy.start()
                deep[color, d, e] = copy
                sent.append(copy)

    forwarded = []
    for e in (0, 1, 3, 2):
        for color, order in enumerate(ORDERS):
            lo, n = thirds[color]
            origin = pos
            if e:
                for d in range(4):
                    deep[color, d, e].wait_recv()
                origin = moved(pos, order[0], 4 - e)
            at = region(origin, order[:1]) + (slice(None), pl.ds(lo, n))
            copy = remote(whole.at[at], whole.at[at], fwd_send.at[color, e], fwd_recv.at[color, e], twin)
            copy.start()
            forwarded.append(copy)
    for copy in forwarded:
        copy.wait_recv()
    sent += forwarded
    for store in stores:
        store.wait()
    for copy in sent:
        copy.wait_send()


def landings(rows, widths):
    return [
        *[pltpu.VMEM((3, 4, 4, rows, n), F32) for n in widths],
        *[pltpu.VMEM((3, 4, rows, n), F32) for n in widths],
        *[pltpu.VMEM((3, rows, n), F32) for n in widths],
    ]


IN_VMEM = pl.BlockSpec(memory_space=pltpu.VMEM)
IN_HBM = pl.BlockSpec(memory_space=pl.ANY)


def fit(visited, phases, proj, frames, targets):
    return pl.pallas_call(
        fit_kernel,
        out_shape=(
            jax.ShapeDtypeStruct((2, 4, 4, 4, 16, 1024), F32),
            jax.ShapeDtypeStruct((1024, 1024), BF16),
            jax.ShapeDtypeStruct((1024, 1024), BF16),
        ),
        in_specs=[pl.BlockSpec(memory_space=pltpu.SMEM), IN_VMEM, IN_HBM, IN_HBM, IN_HBM],
        out_specs=(IN_HBM, IN_HBM, IN_HBM),
        scratch_shapes=[
            pltpu.VMEM((1024, 1024), BF16),
            pltpu.VMEM((1024, 1024), BF16),
            pltpu.VMEM((440, FEATS), F32),
            pltpu.VMEM((440, 1024), F32),
            pltpu.VMEM((440, 1024), BF16),
            pltpu.VMEM((440, 1024), BF16),
            pltpu.VMEM((440, FEATS), BF16),
            pltpu.VMEM((440, FEATS), BF16),
            pltpu.VMEM((1024, 2048), F32),
            pltpu.VMEM((2, 4, 4, 4, 8, FEATS), F32),
            pltpu.VMEM((4, 4, 4, 8, FEATS), F32),
            pltpu.VMEM((2, 4, 4, 4, 8, FEATS), F32),
            pltpu.VMEM((2, 4, 4, 4, 8, 768), F32),
            pltpu.VMEM((4, 4, 4, 8, 768), F32),
            pltpu.VMEM((4, 4, 4, 8, 768), F32),
            pltpu.VMEM((STEPS, FEATS, FEATS), F32),
            pltpu.VMEM((STEPS, FEATS, FEATS), F32),
            pltpu.VMEM((2, FEATS, 256), F32),
            pltpu.VMEM((128, FEATS), F32),
            pltpu.VMEM((FEATS, 128), F32),
            pltpu.VMEM((2, 4, 4, 4, 16, 1024), F32),
            pltpu.VMEM((4, 4, 4, 16, 1024), F32),
            pltpu.VMEM((16, 1024), F32),
            *landings(8, (128, 128, 256)),
            *landings(8, (256, 256, 256)),
            *landings(16, (384, 384, 256)),
            *[pltpu.SemaphoreType.DMA((3, 3, 3)) for _ in range(12)],
            pltpu.SemaphoreType.DMA((6,)),
            pltpu.SemaphoreType.DMA((6,)),
            pltpu.SemaphoreType.DMA((4, 4)),
            pltpu.SemaphoreType.DMA((4, 4)),
            pltpu.SemaphoreType.DMA((3, 4, 3)),
            pltpu.SemaphoreType.DMA((3, 4, 3)),
            pltpu.SemaphoreType.DMA((6,)),
        ],
        compiler_params=pltpu.CompilerParams(
            collective_id=1, has_side_effects=True, vmem_limit_bytes=60 << 20
        ),
    )(visited, phases, proj, frames, targets)


def residual_kernel(targets, solved, fh, fl, residual, weights):
    columns = [solved[:, s * FEATS : (s + 1) * FEATS].T for s in range(STEPS)]
    fitted = dot3((fh[...], fl[...]), halves(jnp.concatenate(columns, axis=0)), NN)
    residual[...] = targets[...] - fitted
    for s in range(STEPS):
        weights[s] = columns[s]


def residual_of(targets, solved, fh, fl):
    n = 512
    return pl.pallas_call(
        residual_kernel,
        grid=(2048 // n,),
        out_shape=(
            jax.ShapeDtypeStruct((1024, 2048), F32),
            jax.ShapeDtypeStruct((STEPS, FEATS, 2048), F32),
        ),
        in_specs=[
            pl.BlockSpec((1024, n), lambda i: (0, i)),
            pl.BlockSpec((n, 1024), lambda i: (i, 0)),
            IN_VMEM,
            IN_VMEM,
        ],
        out_specs=(
            pl.BlockSpec((1024, n), lambda i: (0, i)),
            pl.BlockSpec((STEPS, FEATS, n), lambda i: (0, 0, i)),
        ),
        compiler_params=pltpu.CompilerParams(vmem_limit_bytes=60 << 20),
    )(targets, solved, fh, fl)


def per_device(frames, targets, projection, phases, block_order):
    solved, fh, fl = fit(block_order, phases, projection[0], frames.T, targets)
    return residual_of(targets, solved.reshape(2048, 1024), fh, fl)


def solution(mesh):
    return jax.shard_map(
        per_device,
        mesh=mesh,
        in_specs=(
            P(("wide", "narrow"), None),
            P(("wide", "narrow"), None),
            P(("wide", "narrow"), None, None),
            P(("wide", "narrow"), None),
            P(),
        ),
        out_specs=(P(("wide", "narrow"), None), P()),
        check_vma=False,
    )
```
